32 devices in a mesh: wide: 16 (over z, x, core), narrow: 2 (over y).
Axes of the slice: x: 2, y: 2, z: 4, core: 2. Of those that a mesh axis runs over, the one named last changes fastest.
Arguments:
- tokens: bfloat16 [65536, 384], P(('wide', 'narrow')), may hold values from -6 to 6
- counts: int32 [1024], P(('wide', 'narrow')), may hold values from 13 to 64, as said below
- cotangent: bfloat16 [65536, 384], P(('wide', 'narrow')), may hold values from -6 to 6
- master: float32 [1773312], P(('wide', 'narrow')), as said below
- first: float32 [1773312], P(('wide', 'narrow')), as said below
- second: float32 [1773312], P(('wide', 'narrow')), as said below
- rate: float32 [1], replicated, may hold values from 0.5 to 1
- step: int32 [1], replicated, may hold values from 2 to 20
Outputs:
- layer_out: bfloat16 [65536, 384], P(('wide', 'narrow'))
- grad_input: bfloat16 [65536, 384], P(('wide', 'narrow'))
- master_new: float32 [1773312], P(('wide', 'narrow'))
- first_new: float32 [1773312], P(('wide', 'narrow'))
- second_new: float32 [1773312], P(('wide', 'narrow'))
- copy_new: bfloat16 [1773312], P(('wide', 'narrow'))
The draws below stay inside these ranges and needn't reach their ends.
Inputs may be any that keep to these rules, and one draw needn't show every extreme that they name: The visible patches of a sample are its first counts[s] slots; the others are padding. `master`: master parameters laid out as in the reference program. `first`: first moments of both signs. `second`: second moments, all positive.
All inputs are finite; a program needn't handle non-finite values.
Results may differ from the reference program's by a relative error of at most 0.007.
The reference program's roundings to bfloat16 on the way count: a program that leaves them out, or rounds other values in their place, can miss the bound.
Values may be sent and summed in bfloat16 or wider, within the bound.
No kernel may reach another device: no remote copies, remote signals or barrier semaphores. Data moves between devices by JAX's collectives and lax.ppermute only.
A program may use at most 192 MiB of HBM per device.

```python
import jax
import jax.numpy as jnp
from jax import lax

D = 384
FF = 1536
HEADS = 6
HEAD_DIM = 64
PATCHES = 64
SAMPLES = 1024
TOKENS = 65536
PARAMS = 1773312


def layout_bounds():
    bound_one = 3 * D * D
    bound_two = bound_one + D * D
    bound_three = bound_two + D * FF
    bound_four = bound_three + FF * D
    return (bound_one, bound_two, bound_three, bound_four)


def spread_scale(position):
    bound_one, bound_two, bound_three, bound_four = layout_bounds()
    return jnp.where(position < bound_one, D ** (-0.5), jnp.where(position < bound_two, (D // 8) ** (-0.5), jnp.where(position < bound_three, D ** (-0.5), jnp.where(position < bound_four, FF ** (-0.5), 0.1))))


def gradient_square(position):
    bound_one, bound_two, bound_three, bound_four = layout_bounds()
    offset = position - bound_four
    vector_part = jnp.where(offset < 2 * D, 24.0, jnp.where(offset < 3 * D, 40.0, jnp.where(offset < 5 * D, 14.0, jnp.where(offset < 5 * D + FF, 4.0, 40.0))))
    matrix_part = jnp.where(position < bound_one, 8.0, jnp.where(position < bound_two, 2.0, jnp.where(position < bound_three, 4.0, 16.0)))
    factor = jnp.where(position < bound_four, matrix_part, vector_part)
    return factor * jnp.float32(SAMPLES)


def draw_master(key, part):
    position = jnp.arange(PARAMS, dtype=jnp.int32)
    base = jnp.clip(jax.random.normal(key, (PARAMS,), jnp.float32), -4.0, 4.0)
    offset = position - layout_bounds()[3]
    gains = (offset >= 0) & (offset < D) | (offset >= 3 * D) & (offset < 4 * D)
    return jnp.where(gains, 1.0 + 0.1 * base, spread_scale(position) * base).astype(jnp.float32)


def draw_first(key, part):
    position = jnp.arange(PARAMS, dtype=jnp.int32)
    base = jnp.clip(jax.random.normal(key, (PARAMS,), jnp.float32), -4.0, 4.0)
    return (jnp.sqrt(gradient_square(position)) * base).astype(jnp.float32)


def draw_second(key, part):
    position = jnp.arange(PARAMS, dtype=jnp.int32)
    factor = jnp.exp(jax.random.uniform(key, (PARAMS,), jnp.float32, jnp.log(0.5), jnp.log(8.0)))
    return (gradient_square(position) * factor).astype(jnp.float32)


def draw_counts(key, part):
    drawn = jax.random.randint(key, (SAMPLES,), 13, 65, dtype=jnp.int32)
    return drawn.at[0].set(64).at[1].set(13)


def block_scale(stream_key, dims, cuts, smallest, high):
    factor_of = 1.0
    for dim, parts in cuts:
        heights = jax.random.uniform(jax.random.fold_in(jax.random.fold_in(stream_key, 6), dim), (parts,), jnp.float32, smallest / len(cuts), high / len(cuts))
        factor_of = factor_of * jnp.repeat(jnp.exp(heights), dims[dim] // parts).reshape((-1,) + (1,) * (len(dims) - 1 - dim))
    return factor_of


def centred(stream_key, dims, deviation, most, cuts=(), held_as=jnp.bfloat16):
    level = block_scale(stream_key, dims, cuts, -0.22, 0.18) if cuts else 1.0
    values = jax.random.normal(stream_key, dims, jnp.float32) * deviation * level
    return jnp.minimum(jnp.maximum(values, -most), most).astype(held_as)


def setup_inputs(seed: int = 0) -> dict:
    splits = jax.random.split(jax.random.key(seed), 9)
    tokens = centred(splits[0], (TOKENS, D), 1.0, 6.0, ((0, 32),))
    counts = draw_counts(jax.random.fold_in(splits[8], 71), 0)
    cotangent = centred(splits[2], (TOKENS, D), 1.0, 6.0, ((0, 32),))
    master = draw_master(jax.random.fold_in(splits[8], 71), 0)
    first = draw_first(jax.random.fold_in(splits[8], 71), 0)
    second = draw_second(jax.random.fold_in(splits[8], 71), 0)
    rate = jnp.clip(jax.random.uniform(splits[6], (1,), jnp.float32, 0.5, 1.0), 0.5, 1.0)
    step = jax.random.randint(splits[7], (1,), 2, 21).astype(jnp.int32)
    return dict(tokens=tokens, counts=counts, cotangent=cotangent, master=master, first=first, second=second, rate=rate, step=step)


@jax.custom_vjp
def low(v):
    return lax.optimization_barrier(v.astype(jnp.bfloat16)).astype(jnp.float32)

@jax.custom_vjp
def low_back(v):
    return v

def low_keep(v):
    return (low(v), None)

def low_pass(kept, grad):
    return (grad,)

def back_keep(v):
    return (v, None)

def back_low(kept, grad):
    return (low(grad),)
low.defvjp(low_keep, low_pass)
low_back.defvjp(back_keep, back_low)
highest = lax.Precision.HIGHEST

def matmul(left, right):
    return jnp.dot(left, right, precision=highest, preferred_element_type=jnp.float32)

def layer_norm(values, gain, shift):
    center = values - lax.optimization_barrier(jnp.mean(values, axis=-1, keepdims=True))
    spread = lax.optimization_barrier(jnp.mean(center * center, axis=-1, keepdims=True))
    return center * lax.rsqrt(spread + 1e-06) * gain + shift

def exact_gelu(values):
    return jax.nn.gelu(values, approximate=False)

def bounds():
    bound_one = 3 * D * D
    bound_two = bound_one + D * D
    bound_three = bound_two + D * FF
    bound_four = bound_three + FF * D
    return (bound_one, bound_two, bound_three, bound_four)

def unpack_params(params):
    bound_one, bound_two, bound_three, bound_four = bounds()
    w_qkv = params[:bound_one].reshape(D, 3 * D)
    w_out = params[bound_one:bound_two].reshape(D, D)
    w_up = params[bound_two:bound_three].reshape(D, FF)
    w_down = params[bound_three:bound_four].reshape(FF, D)
    vectors = params[bound_four:]
    return (w_qkv, w_out, w_up, w_down, vectors[:D], vectors[D:2 * D], vectors[2 * D:3 * D], vectors[3 * D:4 * D], vectors[4 * D:5 * D], vectors[5 * D:5 * D + FF], vectors[5 * D + FF:])

def step_scale(position):
    bound_one, bound_two, bound_three, bound_four = bounds()
    scale = jnp.where(position < bound_one, D ** (-0.5), jnp.where(position < bound_two, (D // 8) ** (-0.5), jnp.where(position < bound_three, D ** (-0.5), jnp.where(position < bound_four, FF ** (-0.5), 0.1))))
    decay = jnp.where(position < bound_four, 0.05, 0.0)
    return (scale, decay)

def forward(inputs, group_counts, params):
    w_qkv, w_out, w_up, w_down, gain_one, shift_one, bias_out, gain_two, shift_two, bias_up, bias_down = unpack_params(params)
    samples = group_counts.shape[0]
    normed = low(layer_norm(inputs, gain_one, shift_one))
    packed = low(low_back(matmul(normed, w_qkv)))
    packed = packed.reshape(samples, PATCHES, 3, HEADS, HEAD_DIM)
    queries = packed[:, :, 0]
    keys = packed[:, :, 1]
    values = packed[:, :, 2]
    scores = low_back(jnp.einsum('sqhd,skhd->shqk', queries, keys, precision=highest) * HEAD_DIM ** (-0.5))
    visible = jnp.arange(PATCHES, dtype=jnp.int32)[None, :] < group_counts[:, None]
    scores = jnp.where(visible[:, None, None, :], scores, -1e+30)
    attend = low(jax.nn.softmax(scores, axis=-1))
    mixed = jnp.einsum('shqk,skhd->sqhd', attend, values, precision=highest).reshape(samples * PATCHES, D)
    mixed = low(low_back(mixed))
    hidden_one = inputs + low_back(matmul(mixed, w_out) + bias_out)
    normed_two = low(layer_norm(hidden_one, gain_two, shift_two))
    upward = low_back(matmul(normed_two, w_up) + bias_up)
    active = low(exact_gelu(upward))
    return hidden_one + low_back(matmul(active, w_down) + bias_down)

def reference(tokens, counts, cotangent, master, first, second, rate, step):
    params = lax.optimization_barrier(master.astype(jnp.bfloat16)).astype(jnp.float32)
    group = min(64, SAMPLES)
    groups = SAMPLES // group
    inputs = tokens.astype(jnp.float32).reshape(groups, group * PATCHES, D)
    backs = cotangent.astype(jnp.float32).reshape(groups, group * PATCHES, D)
    group_counts = counts.reshape(groups, group)

    def one_group(summed, item):
        inputs_g, counts_g, backs_g = item
        result, pull = jax.vjp(lambda a, b: forward(a, counts_g, b), inputs_g, params)
        visible = (jnp.arange(PATCHES, dtype=jnp.int32)[None, :] < counts_g[:, None]).reshape(-1, 1)
        grad_in, grad_params = pull(backs_g * visible.astype(jnp.float32))
        return (summed + grad_params, (result.astype(jnp.bfloat16), grad_in.astype(jnp.bfloat16)))
    gradient, (results, grads_in) = lax.scan(one_group, jnp.zeros((PARAMS,), jnp.float32), (inputs, group_counts, backs))
    first_new = 0.5 * first + 0.5 * gradient
    second_new = 0.5 * second + 0.5 * gradient * gradient
    correct = 1.0 - jnp.power(jnp.float32(0.5), step[0].astype(jnp.float32))
    scale, decay = step_scale(jnp.arange(PARAMS, dtype=jnp.int32))
    moved = first_new / correct / (jnp.sqrt(second_new / correct) + 1e-08)
    master_new = master - rate[0] * scale * (moved + decay * master)
    return (results.reshape(TOKENS, D), grads_in.reshape(TOKENS, D), master_new, first_new, second_new, master_new.astype(jnp.bfloat16))
```

```python
import functools

import jax
import jax.numpy as jnp
from jax import lax
from jax.experimental import pallas as pl
from jax.experimental.pallas import tpu as pltpu
from jax.sharding import PartitionSpec as P

D = 384
FF = 1536
HEADS = 6
HEAD_DIM = 64
PATCHES = 64
LANES = 128
PAIRS = HEADS // 2
EPS = 1e-06
AXES = ("wide", "narrow")
QKV_ROWS = 3 * D * D // LANES
OUT_ROWS = D * D // LANES
UP_ROWS = D * FF // LANES
VEC_ROWS = (6 * D + FF) // LANES
FLAT_ROWS = QKV_ROWS + OUT_ROWS + 2 * UP_ROWS + VEC_ROWS
BASE_OUT = QKV_ROWS
BASE_UP = BASE_OUT + OUT_ROWS
BASE_DOWN = BASE_UP + UP_ROWS
BASE_VEC = BASE_DOWN + UP_ROWS
VECTORS = ("gain_one", "shift_one", "bias_out", "gain_two", "shift_two", "bias_up", "bias_down")
VMEM_LIMIT = 60 * 1024 * 1024


def round_up(value, step):
    return (value + step - 1) // step * step


def chunk_shape(shard):
    return round_up(shard + 1024, 16 * LANES) // LANES


def dot(left, right, left_dim, right_dim):
    return lax.dot_general(
        left, right, (((left_dim,), (right_dim,)), ((), ())), preferred_element_type=jnp.float32
    )


def vector_width(name):
    return FF if name == "bias_up" else D


def vector_row(name):
    return VECTORS.index(name)


def unpack_kernel(shard, devices, chunks, w_qkv, w_out, w_up, w_down, vectors, flat):
    rows = chunks.shape[1]
    for owner in range(devices):
        start = owner * shard // 1024 * 8
        piece = chunks[owner].astype(jnp.float32)
        if owner == 0:
            flat[pl.ds(start, rows), :] = piece
        else:
            flat[pl.ds(start, 8), :] = flat[pl.ds(start, 8), :] + piece[:8]
            flat[pl.ds(start + 8, rows - 8), :] = piece[8:]
    for ref, base in ((w_qkv, 0), (w_out, BASE_OUT), (w_up, BASE_UP), (w_down, BASE_DOWN)):
        height, width = ref.shape
        blocks = width // LANES
        for block in range(blocks):
            ref[:, block * LANES : (block + 1) * LANES] = flat[
                pl.ds(base + block, height, stride=blocks), :
            ].astype(jnp.bfloat16)
    row = BASE_VEC
    for index, name in enumerate(VECTORS):
        for block in range(vector_width(name) // LANES):
            vectors[index : index + 1, block * LANES : (block + 1) * LANES] = flat[
                row : row + 1, :
            ]
            row += 1


def unpack(chunks, shard, devices):
    rows = chunks.shape[1]
    flat_rows = max((devices - 1) * shard // 1024 * 8 + rows, round_up(FLAT_ROWS, 8))
    low = jnp.bfloat16
    return pl.pallas_call(
        functools.partial(unpack_kernel, shard, devices),
        name="unpack",
        out_shape=(
            jax.ShapeDtypeStruct((D, 3 * D), low),
            jax.ShapeDtypeStruct((D, D), low),
            jax.ShapeDtypeStruct((D, FF), low),
            jax.ShapeDtypeStruct((FF, D), low),
            jax.ShapeDtypeStruct((8, FF), jnp.float32),
        ),
        scratch_shapes=[pltpu.VMEM((flat_rows, LANES), jnp.float32)],
        compiler_params=pltpu.CompilerParams(vmem_limit_bytes=VMEM_LIMIT),
    )(chunks)


def vector(vectors, name):
    index = vector_row(name)
    return vectors[index : index + 1, : vector_width(name)]


def normalize(values):
    center = values - jnp.mean(values, axis=-1, keepdims=True)
    spread = jnp.mean(center * center, axis=-1, keepdims=True)
    scale = lax.rsqrt(spread + EPS)
    return center * scale, scale


def norm_back(grad, gain, hat, scale):
    inner = grad * gain
    mean_inner = jnp.mean(inner, axis=-1, keepdims=True)
    mean_cross = jnp.mean(inner * hat, axis=-1, keepdims=True)
    return scale * (inner - mean_inner - hat * mean_cross)


def column_sum(values):
    return jnp.sum(values, axis=0, keepdims=True)


def pair_lanes(rows):
    return lax.broadcasted_iota(jnp.int32, (rows, LANES), 1)


def block_diagonal(values, first_half):
    zero = jnp.zeros_like(values)
    return jnp.concatenate(
        [jnp.where(first_half, values, zero), jnp.where(first_half, zero, values)], axis=0
    )


def spread_halves(reduce, values, first_half, fill):
    first = reduce(jnp.where(first_half, values, fill), axis=-1, keepdims=True)
    second = reduce(jnp.where(first_half, fill, values), axis=-1, keepdims=True)
    return jnp.where(first_half, first, second)


def attention_kernel(
    counts, tokens, w_qkv, w_out, vectors, packed, chance, mixed, hidden
):
    block_rows = tokens.shape[0]
    samples = block_rows // PATCHES
    first_sample = pl.program_id(0) * samples
    inputs = tokens[...].astype(jnp.float32)
    hat, _ = normalize(inputs)
    normed = hat * vector(vectors, "gain_one") + vector(vectors, "shift_one")
    packed[...] = dot(normed.astype(jnp.bfloat16), w_qkv[...], 1, 0).astype(jnp.bfloat16)
    lanes = pair_lanes(PATCHES)
    first_half = lanes < HEAD_DIM
    keys_at = lanes % HEAD_DIM
    for sample in range(samples):
        rows = slice(sample * PATCHES, (sample + 1) * PATCHES)
        visible = keys_at < counts[first_sample + sample]
        for pair in range(PAIRS):
            at = pair * LANES
            queries = packed[rows, at : at + LANES]
            keys = block_diagonal(packed[rows, D + at : D + at + LANES], first_half)
            values = block_diagonal(packed[rows, 2 * D + at : 2 * D + at + LANES], first_half)
            scores = dot(queries, keys, 1, 1) * HEAD_DIM**-0.5
            scores = jnp.where(visible, scores, -1e30)
            largest = spread_halves(jnp.max, scores, first_half, -jnp.inf)
            exponent = jnp.exp(scores - largest)
            total = spread_halves(jnp.sum, exponent, first_half, 0.0)
            attend = exponent / total
            chance[rows, at : at + LANES] = attend
            mixed[rows, at : at + LANES] = dot(attend.astype(jnp.bfloat16), values, 1, 0).astype(
                jnp.bfloat16
            )
    hidden[...] = inputs + dot(mixed[...], w_out[...], 1, 0) + vector(vectors, "bias_out")


def attention(counts, tokens, w_qkv, w_out, vectors, block):
    rows = tokens.shape[0]

    def by_rows(width):
        return pl.BlockSpec((block, width), lambda i, counts: (i, 0))

    def whole(array):
        return pl.BlockSpec(array.shape, lambda i, counts: (0, 0))

    return pl.pallas_call(
        attention_kernel,
        name="attention",
        grid_spec=pltpu.PrefetchScalarGridSpec(
            num_scalar_prefetch=1,
            grid=(rows // block,),
            in_specs=[by_rows(D), whole(w_qkv), whole(w_out), whole(vectors)],
            out_specs=[by_rows(3 * D), by_rows(D), by_rows(D), by_rows(D)],
        ),
        out_shape=(
            jax.ShapeDtypeStruct((rows, 3 * D), jnp.bfloat16),
            jax.ShapeDtypeStruct((rows, D), jnp.float32),
            jax.ShapeDtypeStruct((rows, D), jnp.bfloat16),
            jax.ShapeDtypeStruct((rows, D), jnp.float32),
        ),
        compiler_params=pltpu.CompilerParams(vmem_limit_bytes=VMEM_LIMIT),
    )(counts, tokens, w_qkv, w_out, vectors)


def visible_rows(counts, first_sample, samples):
    slots = lax.broadcasted_iota(jnp.int32, (PATCHES, 1), 0)
    return jnp.concatenate(
        [
            jnp.where(slots < counts[first_sample + sample], 1.0, 0.0)
            for sample in range(samples)
        ],
        axis=0,
    )


def feed_kernel(
    step_columns,
    counts,
    hidden,
    cotangent,
    w_up,
    w_down,
    vectors,
    result,
    grad_hidden,
    grad_up,
    grad_down,
    grad_vectors,
    acc_up,
    acc_down,
):
    step = pl.program_id(0)
    block_rows = hidden.shape[0]
    samples = block_rows // PATCHES

    @pl.when(step == 0)
    def _():
        acc_up[...] = jnp.zeros_like(acc_up)
        acc_down[...] = jnp.zeros_like(acc_down)
        grad_vectors[...] = jnp.zeros_like(grad_vectors)

    def add_vector(name, values):
        index = vector_row(name)
        width = vector_width(name)
        grad_vectors[index : index + 1, :width] += column_sum(values)

    through = hidden[...]
    hat, scale = normalize(through)
    gain = vector(vectors, "gain_two")
    normed = (hat * gain + vector(vectors, "shift_two")).astype(jnp.bfloat16)
    grad_out = cotangent[...].astype(jnp.float32) * visible_rows(counts, step * samples, samples)
    grad_out_low = grad_out.astype(jnp.bfloat16)
    add_vector("bias_down", grad_out)
    total = through + vector(vectors, "bias_down")
    grad_normed = jnp.zeros_like(through)
    bias_up = vector(vectors, "bias_up")
    for at in range(0, FF, step_columns):
        columns = slice(at, at + step_columns)
        upward = dot(normed, w_up[:, columns], 1, 0) + bias_up[:, columns]
        below = 0.5 * (1.0 + lax.erf(upward * 0.5**0.5))
        active = (upward * below).astype(jnp.bfloat16)
        slope = below + upward * (jnp.exp(-0.5 * upward * upward) * (0.5 / jnp.pi) ** 0.5)
        total = total + dot(active, w_down[columns, :], 1, 0)
        grad_upward = dot(grad_out_low, w_down[columns, :], 1, 1) * slope
        grad_upward_low = grad_upward.astype(jnp.bfloat16)
        grad_vectors[5:6, columns] += column_sum(grad_upward_low.astype(jnp.float32))
        acc_down[columns, :] += dot(active, grad_out_low, 0, 0)
        acc_up[:, columns] += dot(normed, grad_upward_low, 0, 0)
        grad_normed = grad_normed + dot(grad_upward_low, w_up[:, columns], 1, 1)
    result[...] = total.astype(jnp.bfloat16)
    add_vector("gain_two", grad_normed * hat)
    add_vector("shift_two", grad_normed)
    grad_hidden[...] = grad_out + norm_back(grad_normed, gain, hat, scale)

    @pl.when(step == pl.num_programs(0) - 1)
    def _():
        flatten(acc_up, grad_up, 0)
        flatten(acc_down, grad_down, 0)


def flatten(matrix, flat, base):
    height, width = matrix.shape
    blocks = width // LANES
    for block in range(blocks):
        flat[pl.ds(base + block, height, stride=blocks), :] = matrix[
            :, block * LANES : (block + 1) * LANES
        ]


def feed(counts, hidden, cotangent, w_up, w_down, vectors, block, step_columns):
    rows = hidden.shape[0]

    def by_rows(width):
        return pl.BlockSpec((block, width), lambda i, counts: (i, 0))

    def whole(shape):
        return pl.BlockSpec(shape, lambda i, counts: (0, 0))

    return pl.pallas_call(
        functools.partial(feed_kernel, step_columns),
        name="feed",
        grid_spec=pltpu.PrefetchScalarGridSpec(
            num_scalar_prefetch=1,
            grid=(rows // block,),
            in_specs=[by_rows(D), by_rows(D), whole(w_up.shape), whole(w_down.shape), whole(vectors.shape)],
            out_specs=[by_rows(D), by_rows(D), whole((UP_ROWS, LANES)), whole((UP_ROWS, LANES)), whole((8, FF))],
            scratch_shapes=[pltpu.VMEM((D, FF), jnp.float32), pltpu.VMEM((FF, D), jnp.float32)],
        ),
        out_shape=(
            jax.ShapeDtypeStruct((rows, D), jnp.bfloat16),
            jax.ShapeDtypeStruct((rows, D), jnp.float32),
            jax.ShapeDtypeStruct((UP_ROWS, LANES), jnp.float32),
            jax.ShapeDtypeStruct((UP_ROWS, LANES), jnp.float32),
            jax.ShapeDtypeStruct((8, FF), jnp.float32),
        ),
        compiler_params=pltpu.CompilerParams(vmem_limit_bytes=VMEM_LIMIT),
    )(counts, hidden, cotangent, w_up, w_down, vectors)


def attention_back_kernel(
    tokens,
    packed,
    chance,
    mixed,
    grad_hidden,
    w_qkv,
    w_out,
    vectors,
    grad_input,
    grad_qkv,
    grad_w_out,
    grad_vectors,
    acc_qkv,
    acc_out,
    grad_packed,
):
    step = pl.program_id(0)
    samples = tokens.shape[0] // PATCHES

    @pl.when(step == 0)
    def _():
        acc_qkv[...] = jnp.zeros_like(acc_qkv)
        acc_out[...] = jnp.zeros_like(acc_out)
        grad_vectors[...] = jnp.zeros_like(grad_vectors)

    def add_vector(name, values):
        index = vector_row(name)
        grad_vectors[index : index + 1, :D] += column_sum(values)

    grad_through = grad_hidden[...]
    grad_low = grad_through.astype(jnp.bfloat16)
    add_vector("bias_out", grad_low.astype(jnp.float32))
    acc_out[...] += dot(mixed[...], grad_low, 0, 0)
    grad_mixed = dot(grad_low, w_out[...], 1, 1).astype(jnp.bfloat16)
    first_half = pair_lanes(PATCHES) < HEAD_DIM
    factor = HEAD_DIM**-0.5
    for sample in range(samples):
        rows = slice(sample * PATCHES, (sample + 1) * PATCHES)
        for pair in range(PAIRS):
            at = pair * LANES
            queries = packed[rows, at : at + LANES]
            keys = block_diagonal(packed[rows, D + at : D + at + LANES], first_half)
            values = block_diagonal(packed[rows, 2 * D + at : 2 * D + at + LANES], first_half)
            attend = chance[rows, at : at + LANES]
            grad_pair = grad_mixed[rows, at : at + LANES]
            grad_attend = dot(grad_pair, values, 1, 1)
            inner = spread_halves(jnp.sum, attend * grad_attend, first_half, 0.0)
            grad_scores = (attend * (grad_attend - inner)).astype(jnp.bfloat16)
            grad_queries = dot(grad_scores, keys, 1, 0) * factor
            grad_keys = dot(grad_scores, queries, 0, 0)
            grad_keys = jnp.where(first_half, grad_keys[:PATCHES], grad_keys[PATCHES:]) * factor
            grad_values = dot(attend.astype(jnp.bfloat16), grad_pair, 0, 0)
            grad_values = jnp.where(first_half, grad_values[:PATCHES], grad_values[PATCHES:])
            grad_packed[rows, at : at + LANES] = grad_queries.astype(jnp.bfloat16)
            grad_packed[rows, D + at : D + at + LANES] = grad_keys.astype(jnp.bfloat16)
            grad_packed[rows, 2 * D + at : 2 * D + at + LANES] = grad_values.astype(jnp.bfloat16)
    hat, scale = normalize(tokens[...].astype(jnp.float32))
    gain = vector(vectors, "gain_one")
    normed = (hat * gain + vector(vectors, "shift_one")).astype(jnp.bfloat16)
    acc_qkv[...] += dot(normed, grad_packed[...], 0, 0)
    grad_normed = dot(grad_packed[...], w_qkv[...], 1, 1)
    add_vector("gain_one", grad_normed * hat)
    add_vector("shift_one", grad_normed)
    grad_input[...] = (grad_through + norm_back(grad_normed, gain, hat, scale)).astype(
        jnp.bfloat16
    )

    @pl.when(step == pl.num_programs(0) - 1)
    def _():
        flatten(acc_qkv, grad_qkv, 0)
        flatten(acc_out, grad_w_out, 0)


def attention_back(tokens, packed, chance, mixed, grad_hidden, w_qkv, w_out, vectors, block):
    rows = tokens.shape[0]

    def by_rows(width):
        return pl.BlockSpec((block, width), lambda i: (i, 0))

    def whole(shape):
        return pl.BlockSpec(shape, lambda i: (0, 0))

    return pl.pallas_call(
        attention_back_kernel,
        name="attention_back",
        grid=(rows // block,),
        in_specs=[
            by_rows(D),
            by_rows(3 * D),
            by_rows(D),
            by_rows(D),
            by_rows(D),
            whole(w_qkv.shape),
            whole(w_out.shape),
            whole(vectors.shape),
        ],
        out_specs=[by_rows(D), whole((QKV_ROWS, LANES)), whole((OUT_ROWS, LANES)), whole((8, FF))],
        scratch_shapes=[
            pltpu.VMEM((D, 3 * D), jnp.float32),
            pltpu.VMEM((D, D), jnp.float32),
            pltpu.VMEM((block, 3 * D), jnp.bfloat16),
        ],
        out_shape=(
            jax.ShapeDtypeStruct((rows, D), jnp.bfloat16),
            jax.ShapeDtypeStruct((QKV_ROWS, LANES), jnp.float32),
            jax.ShapeDtypeStruct((OUT_ROWS, LANES), jnp.float32),
            jax.ShapeDtypeStruct((8, FF), jnp.float32),
        ),
        compiler_params=pltpu.CompilerParams(vmem_limit_bytes=VMEM_LIMIT),
    )(tokens, packed, chance, mixed, grad_hidden, w_qkv, w_out, vectors)


def pack_kernel(shard, devices, grad_qkv, grad_out, grad_up, grad_down, vectors, chunks, flat):
    rows = chunks.shape[1]
    flat[0:QKV_ROWS, :] = grad_qkv[...]
    flat[BASE_OUT : BASE_OUT + OUT_ROWS, :] = grad_out[...]
    flat[BASE_UP : BASE_UP + UP_ROWS, :] = grad_up[...]
    flat[BASE_DOWN : BASE_DOWN + UP_ROWS, :] = grad_down[...]
    row = BASE_VEC
    for index, name in enumerate(VECTORS):
        for block in range(vector_width(name) // LANES):
            flat[row : row + 1, :] = vectors[
                index : index + 1, block * LANES : (block + 1) * LANES
            ]
            row += 1
    flat[row:, :] = jnp.zeros_like(flat[row:, :])
    for owner in range(devices):
        start = owner * shard // 1024 * 8
        chunks[owner] = flat[start : start + rows, :].astype(jnp.bfloat16)


def pack(grad_qkv, grad_out, grad_up, grad_down, vectors, shard, devices):
    rows = chunk_shape(shard)
    flat_rows = max((devices - 1) * shard // 1024 * 8 + rows, round_up(FLAT_ROWS, 8))
    return pl.pallas_call(
        functools.partial(pack_kernel, shard, devices),
        name="pack",
        out_shape=jax.ShapeDtypeStruct((devices, rows, LANES), jnp.bfloat16),
        scratch_shapes=[pltpu.VMEM((flat_rows, LANES), jnp.float32)],
        compiler_params=pltpu.CompilerParams(vmem_limit_bytes=VMEM_LIMIT),
    )(grad_qkv, grad_out, grad_up, grad_down, vectors)


def step_scale(position):
    bound_one = QKV_ROWS * LANES
    bound_two = BASE_UP * LANES
    bound_three = BASE_DOWN * LANES
    bound_four = BASE_VEC * LANES
    scale = jnp.where(
        position < bound_one,
        D ** (-0.5),
        jnp.where(
            position < bound_two,
            (D // 8) ** (-0.5),
            jnp.where(
                position < bound_three,
                D ** (-0.5),
                jnp.where(position < bound_four, FF ** (-0.5), 0.1),
            ),
        ),
    )
    decay = jnp.where(position < bound_four, 0.05, 0.0)
    return (scale, decay)


def on_device(tokens, counts, cotangent, master, first, second, rate, step):
    shard = master.shape[0]
    devices = lax.axis_size(AXES)
    me = lax.axis_index(AXES)
    rows = chunk_shape(shard)
    offset = me * shard % 1024
    own = lax.dynamic_update_slice(
        jnp.zeros((rows * LANES,), jnp.bfloat16), master.astype(jnp.bfloat16), (offset,)
    ).reshape(rows, LANES)
    chunks = lax.all_gather(lax.all_gather(own, "narrow"), "wide").reshape(devices, rows, LANES)
    w_qkv, w_out, w_up, w_down, vectors = unpack(chunks, shard, devices)
    packed, chance, mixed, hidden = attention(counts, tokens, w_qkv, w_out, vectors, 512)
    result, grad_hidden, grad_up, grad_down, vectors_two = feed(
        counts, hidden, cotangent, w_up, w_down, vectors, 256, 512
    )
    grad_input, grad_qkv, grad_out, vectors_one = attention_back(
        tokens, packed, chance, mixed, grad_hidden, w_qkv, w_out, vectors, 512
    )
    sent = pack(
        grad_qkv, grad_out, grad_up, grad_down, vectors_one + vectors_two, shard, devices
    )
    sent = sent.reshape(lax.axis_size("wide"), lax.axis_size("narrow"), rows, LANES)
    reduced = lax.psum_scatter(
        lax.psum_scatter(sent, "wide", scatter_dimension=0), "narrow", scatter_dimension=0
    )
    reduced = lax.dynamic_slice(
        reduced.astype(jnp.float32).reshape(rows * LANES), (offset,), (shard,)
    )
    position = me * shard + jnp.arange(shard, dtype=jnp.int32)
    first_new = 0.5 * first + 0.5 * reduced
    second_new = 0.5 * second + 0.5 * reduced * reduced
    correct = 1.0 - jnp.power(jnp.float32(0.5), step[0].astype(jnp.float32))
    scale, decay = step_scale(position)
    moved = first_new / correct / (jnp.sqrt(second_new / correct) + 1e-08)
    master_new = master - rate[0] * scale * (moved + decay * master)
    return (
        result,
        grad_input,
        master_new,
        first_new,
        second_new,
        master_new.astype(jnp.bfloat16),
    )


def solution(mesh):
    split = P(AXES)
    by_rows = P(AXES, None)
    return jax.shard_map(
        on_device,
        mesh=mesh,
        in_specs=(by_rows, split, by_rows, split, split, split, P(), P()),
        out_specs=(by_rows, by_rows, split, split, split, split),
        check_vma=False,
    )
```

```python
import functools
import itertools

import jax
import jax.numpy as jnp
from jax import lax
from jax.experimental import pallas as pl
from jax.experimental.pallas import tpu as pltpu
from jax.sharding import PartitionSpec as P
import numpy as np

D = 384
FF = 1536
HEADS = 6
HEAD_DIM = 64
PATCHES = 64
LANES = 128
PAIRS = HEADS // 2
EPS = 1e-06
AXES = ("wide", "narrow")
QKV_ROWS = 3 * D * D // LANES
OUT_ROWS = D * D // LANES
UP_ROWS = D * FF // LANES
VEC_ROWS = (6 * D + FF) // LANES
FLAT_ROWS = QKV_ROWS + OUT_ROWS + 2 * UP_ROWS + VEC_ROWS
BASE_OUT = QKV_ROWS
BASE_UP = BASE_OUT + OUT_ROWS
BASE_DOWN = BASE_UP + UP_ROWS
BASE_VEC = BASE_DOWN + UP_ROWS
VECTORS = ("gain_one", "shift_one", "bias_out", "gain_two", "shift_two", "bias_up", "bias_down")
VMEM_LIMIT = 60 * 1024 * 1024


def round_up(value, step):
    return (value + step - 1) // step * step


def chunk_rows(shard):
    return round_up(shard + 1024, 16 * LANES) // LANES


def dot(left, right, left_dim, right_dim):
    return lax.dot_general(
        left, right, (((left_dim,), (right_dim,)), ((), ())), preferred_element_type=jnp.float32
    )


def vector_width(name):
    return FF if name == "bias_up" else D


def vector_row(name):
    return VECTORS.index(name)


def exchange_plan(wide, narrow):
    devices = wide * narrow
    core = narrow
    bits = [1 << k for k in reversed(range(devices.bit_length() - 1)) if 1 << k != core]
    half = (len(bits) + 1) // 2
    rounds = []
    for first, second in itertools.zip_longest(bits[:half], bits[half:]):
        if second is None:
            rounds.append((first, first))
        else:
            rounds += [(first, second), (second, first)]
    owners = np.zeros((devices, devices), np.int32)
    for device in range(devices):
        for owner in range(devices):
            across = device ^ owner
            holder = device ^ core if across & core else device
            side = 1 if holder & core else 0
            slot = devices // 2 if across & core else 0
            for index, pair in enumerate(rounds):
                if across & pair[side]:
                    slot += 1 << index
            owners[device, slot] = owner
    swaps = [
        [(device, device ^ pair[1 if device & core else 0]) for device in range(devices)]
        for pair in rounds
    ]
    return swaps, [(device, device ^ core) for device in range(devices)], owners


def gather_chunks(own, swaps, core_swap):
    held = own[None]
    for swap in swaps[:-1]:
        held = jnp.concatenate([held, lax.ppermute(held, AXES, swap)], axis=0)
    held_core = lax.ppermute(held, AXES, core_swap)
    taken = lax.ppermute(held, AXES, swaps[-1])
    taken_core = lax.ppermute(taken, AXES, core_swap)
    return held, taken, held_core, taken_core


def scatter_chunks(kept, sent, swaps, core_swap):
    parts = [kept, lax.ppermute(sent, AXES, core_swap)]
    for swap in reversed(swaps):
        half = parts[0].shape[0] // 2
        upper = sum(part[half:].astype(jnp.float32) for part in parts)
        parts = [part[:half] for part in parts]
        parts.append(lax.ppermute(upper.astype(jnp.bfloat16), AXES, swap))
    return sum(part[0].astype(jnp.float32) for part in parts)


def chunk_start(owner, shard):
    return owner * shard // 1024 * 8


def unpack_kernel(shard, starts, *refs):
    pieces, (w_qkv, w_out, w_up, w_down, vectors, flat) = refs[:4], refs[4:]
    rows = pieces[0].shape[1]
    devices = 4 * pieces[0].shape[0]
    sure = shard // 1024 * 8
    for owner in range(devices):
        start = chunk_start(owner, shard)
        flat[start : start + 8, :] = jnp.zeros((8, LANES), jnp.float32)
        flat[start + sure : start + rows, :] = jnp.zeros((rows - sure, LANES), jnp.float32)
    for slot in range(devices):
        source = pieces[slot * 4 // devices]
        piece = source[slot % source.shape[0]].astype(jnp.float32)
        start = pl.multiple_of(starts[slot], 8)
        flat[pl.ds(start, 8), :] += piece[:8]
        flat[pl.ds(start + 8, sure - 8), :] = piece[8:sure]
        flat[pl.ds(start + sure, rows - sure), :] += piece[sure:]
    for ref, base in ((w_qkv, 0), (w_out, BASE_OUT), (w_up, BASE_UP), (w_down, BASE_DOWN)):
        height, width = ref.shape
        blocks = width // LANES
        for block in range(blocks):
            ref[:, block * LANES : (block + 1) * LANES] = flat[
                pl.ds(base + block, height, stride=blocks), :
            ].astype(jnp.bfloat16)
    row = BASE_VEC
    for index, name in enumerate(VECTORS):
        for block in range(vector_width(name) // LANES):
            vectors[index : index + 1, block * LANES : (block + 1) * LANES] = flat[
                row : row + 1, :
            ]
            row += 1


def unpack(starts, pieces, shard):
    quarter, rows, _ = pieces[0].shape
    devices = 4 * quarter
    flat_rows = max(chunk_start(devices - 1, shard) + rows, round_up(FLAT_ROWS, 8))
    low = jnp.bfloat16

    def whole(shape):
        return pl.BlockSpec(shape, lambda i, starts: (0,) * len(shape))

    shapes = ((D, 3 * D), (D, D), (D, FF), (FF, D), (8, FF))
    return pl.pallas_call(
        functools.partial(unpack_kernel, shard),
        name="unpack",
        grid_spec=pltpu.PrefetchScalarGridSpec(
            num_scalar_prefetch=1,
            grid=(1,),
            in_specs=[whole(piece.shape) for piece in pieces],
            out_specs=[whole(shape) for shape in shapes],
            scratch_shapes=[pltpu.VMEM((flat_rows, LANES), jnp.float32)],
        ),
        out_shape=[jax.ShapeDtypeStruct(shape, low) for shape in shapes[:4]]
        + [jax.ShapeDtypeStruct(shapes[4], jnp.float32)],
        compiler_params=pltpu.CompilerParams(vmem_limit_bytes=VMEM_LIMIT),
    )(starts, *pieces)


def vector(vectors, name):
    index = vector_row(name)
    return vectors[index : index + 1, : vector_width(name)]


def normalize(values):
    center = values - jnp.mean(values, axis=-1, keepdims=True)
    spread = jnp.mean(center * center, axis=-1, keepdims=True)
    scale = lax.rsqrt(spread + EPS)
    return center * scale, scale


def norm_back(grad, gain, hat, scale):
    inner = grad * gain
    mean_inner = jnp.mean(inner, axis=-1, keepdims=True)
    mean_cross = jnp.mean(inner * hat, axis=-1, keepdims=True)
    return scale * (inner - mean_inner - hat * mean_cross)


def column_sum(values):
    return jnp.sum(values, axis=0, keepdims=True)


def pair_lanes(rows):
    return lax.broadcasted_iota(jnp.int32, (rows, LANES), 1)


def block_diagonal(values, first_half):
    zero = jnp.zeros_like(values)
    return jnp.concatenate(
        [jnp.where(first_half, values, zero), jnp.where(first_half, zero, values)], axis=0
    )


def spread_halves(reduce, values, first_half, fill):
    first = reduce(jnp.where(first_half, values, fill), axis=-1, keepdims=True)
    second = reduce(jnp.where(first_half, fill, values), axis=-1, keepdims=True)
    return jnp.where(first_half, first, second)


def attention_kernel(
    counts, tokens, w_qkv, w_out, vectors, packed, chance, mixed, hidden
):
    block_rows = tokens.shape[0]
    samples = block_rows // PATCHES
    first_sample = pl.program_id(0) * samples
    inputs = tokens[...].astype(jnp.float32)
    hat, _ = normalize(inputs)
    normed = hat * vector(vectors, "gain_one") + vector(vectors, "shift_one")
    packed[...] = dot(normed.astype(jnp.bfloat16), w_qkv[...], 1, 0).astype(jnp.bfloat16)
    lanes = pair_lanes(PATCHES)
    first_half = lanes < HEAD_DIM
    keys_at = lanes % HEAD_DIM
    for sample in range(samples):
        rows = slice(sample * PATCHES, (sample + 1) * PATCHES)
        visible = keys_at < counts[first_sample + sample]
        for pair in range(PAIRS):
            at = pair * LANES
            queries = packed[rows, at : at + LANES]
            keys = block_diagonal(packed[rows, D + at : D + at + LANES], first_half)
            values = block_diagonal(packed[rows, 2 * D + at : 2 * D + at + LANES], first_half)
            scores = dot(queries, keys, 1, 1) * HEAD_DIM**-0.5
            scores = jnp.where(visible, scores, -1e30)
            largest = spread_halves(jnp.max, scores, first_half, -jnp.inf)
            exponent = jnp.exp(scores - largest)
            total = spread_halves(jnp.sum, exponent, first_half, 0.0)
            attend = exponent / total
            chance[rows, at : at + LANES] = attend
            mixed[rows, at : at + LANES] = dot(attend.astype(jnp.bfloat16), values, 1, 0).astype(
                jnp.bfloat16
            )
    hidden[...] = inputs + dot(mixed[...], w_out[...], 1, 0) + vector(vectors, "bias_out")


def attention(counts, tokens, w_qkv, w_out, vectors, block):
    rows = tokens.shape[0]

    def by_rows(width):
        return pl.BlockSpec((block, width), lambda i, counts: (i, 0))

    def whole(array):
        return pl.BlockSpec(array.shape, lambda i, counts: (0, 0))

    return pl.pallas_call(
        attention_kernel,
        name="attention",
        grid_spec=pltpu.PrefetchScalarGridSpec(
            num_scalar_prefetch=1,
            grid=(rows // block,),
            in_specs=[by_rows(D), whole(w_qkv), whole(w_out), whole(vectors)],
            out_specs=[by_rows(3 * D), by_rows(D), by_rows(D), by_rows(D)],
        ),
        out_shape=(
            jax.ShapeDtypeStruct((rows, 3 * D), jnp.bfloat16),
            jax.ShapeDtypeStruct((rows, D), jnp.float32),
            jax.ShapeDtypeStruct((rows, D), jnp.bfloat16),
            jax.ShapeDtypeStruct((rows, D), jnp.float32),
        ),
        compiler_params=pltpu.CompilerParams(vmem_limit_bytes=VMEM_LIMIT),
    )(counts, tokens, w_qkv, w_out, vectors)


def visible_rows(counts, first_sample, samples):
    slots = lax.broadcasted_iota(jnp.int32, (PATCHES, 1), 0)
    return jnp.concatenate(
        [
            jnp.where(slots < counts[first_sample + sample], 1.0, 0.0)
            for sample in range(samples)
        ],
        axis=0,
    )


def feed_kernel(
    step_columns,
    counts,
    hidden,
    cotangent,
    w_up,
    w_down,
    vectors,
    result,
    grad_hidden,
    grad_up,
    grad_down,
    grad_vectors,
    acc_up,
    acc_down,
):
    step = pl.program_id(0)
    block_rows = hidden.shape[0]
    samples = block_rows // PATCHES

    @pl.when(step == 0)
    def _():
        acc_up[...] = jnp.zeros_like(acc_up)
        acc_down[...] = jnp.zeros_like(acc_down)
        grad_vectors[...] = jnp.zeros_like(grad_vectors)

    def add_vector(name, values):
        index = vector_row(name)
        width = vector_width(name)
        grad_vectors[index : index + 1, :width] += column_sum(values)

    through = hidden[...]
    hat, scale = normalize(through)
    gain = vector(vectors, "gain_two")
    normed = (hat * gain + vector(vectors, "shift_two")).astype(jnp.bfloat16)
    grad_out = cotangent[...].astype(jnp.float32) * visible_rows(counts, step * samples, samples)
    grad_out_low = grad_out.astype(jnp.bfloat16)
    add_vector("bias_down", grad_out)
    total = through + vector(vectors, "bias_down")
    grad_normed = jnp.zeros_like(through)
    bias_up = vector(vectors, "bias_up")
    for at in range(0, FF, step_columns):
        columns = slice(at, at + step_columns)
        upward = dot(normed, w_up[:, columns], 1, 0) + bias_up[:, columns]
        below = 0.5 * (1.0 + lax.erf(upward * 0.5**0.5))
        active = (upward * below).astype(jnp.bfloat16)
        slope = below + upward * (jnp.exp(-0.5 * upward * upward) * (0.5 / jnp.pi) ** 0.5)
        total = total + dot(active, w_down[columns, :], 1, 0)
        grad_upward = dot(grad_out_low, w_down[columns, :], 1, 1) * slope
        grad_upward_low = grad_upward.astype(jnp.bfloat16)
        grad_vectors[5:6, columns] += column_sum(grad_upward_low.astype(jnp.float32))
        acc_down[columns, :] += dot(active, grad_out_low, 0, 0)
        acc_up[:, columns] += dot(normed, grad_upward_low, 0, 0)
        grad_normed = grad_normed + dot(grad_upward_low, w_up[:, columns], 1, 1)
    result[...] = total.astype(jnp.bfloat16)
    add_vector("gain_two", grad_normed * hat)
    add_vector("shift_two", grad_normed)
    grad_hidden[...] = grad_out + norm_back(grad_normed, gain, hat, scale)

    @pl.when(step == pl.num_programs(0) - 1)
    def _():
        flatten(acc_up, grad_up, 0)
        flatten(acc_down, grad_down, 0)


def flatten(matrix, flat, base):
    height, width = matrix.shape
    blocks = width // LANES
    for block in range(blocks):
        flat[pl.ds(base + block, height, stride=blocks), :] = matrix[
            :, block * LANES : (block + 1) * LANES
        ]


def feed(counts, hidden, cotangent, w_up, w_down, vectors, block, step_columns):
    rows = hidden.shape[0]

    def by_rows(width):
        return pl.BlockSpec((block, width), lambda i, counts: (i, 0))

    def whole(shape):
        return pl.BlockSpec(shape, lambda i, counts: (0, 0))

    return pl.pallas_call(
        functools.partial(feed_kernel, step_columns),
        name="feed",
        grid_spec=pltpu.PrefetchScalarGridSpec(
            num_scalar_prefetch=1,
            grid=(rows // block,),
            in_specs=[by_rows(D), by_rows(D), whole(w_up.shape), whole(w_down.shape), whole(vectors.shape)],
            out_specs=[by_rows(D), by_rows(D), whole((UP_ROWS, LANES)), whole((UP_ROWS, LANES)), whole((8, FF))],
            scratch_shapes=[pltpu.VMEM((D, FF), jnp.float32), pltpu.VMEM((FF, D), jnp.float32)],
        ),
        out_shape=(
            jax.ShapeDtypeStruct((rows, D), jnp.bfloat16),
            jax.ShapeDtypeStruct((rows, D), jnp.float32),
            jax.ShapeDtypeStruct((UP_ROWS, LANES), jnp.float32),
            jax.ShapeDtypeStruct((UP_ROWS, LANES), jnp.float32),
            jax.ShapeDtypeStruct((8, FF), jnp.float32),
        ),
        compiler_params=pltpu.CompilerParams(vmem_limit_bytes=VMEM_LIMIT),
    )(counts, hidden, cotangent, w_up, w_down, vectors)


def attention_back_kernel(
    tokens,
    packed,
    chance,
    mixed,
    grad_hidden,
    w_qkv,
    w_out,
    vectors,
    grad_input,
    grad_qkv,
    grad_w_out,
    grad_vectors,
    acc_qkv,
    acc_out,
    grad_packed,
):
    step = pl.program_id(0)
    samples = tokens.shape[0] // PATCHES

    @pl.when(step == 0)
    def _():
        acc_qkv[...] = jnp.zeros_like(acc_qkv)
        acc_out[...] = jnp.zeros_like(acc_out)
        grad_vectors[...] = jnp.zeros_like(grad_vectors)

    def add_vector(name, values):
        index = vector_row(name)
        grad_vectors[index : index + 1, :D] += column_sum(values)

    grad_through = grad_hidden[...]
    grad_low = grad_through.astype(jnp.bfloat16)
    add_vector("bias_out", grad_low.astype(jnp.float32))
    acc_out[...] += dot(mixed[...], grad_low, 0, 0)
    grad_mixed = dot(grad_low, w_out[...], 1, 1).astype(jnp.bfloat16)
    first_half = pair_lanes(PATCHES) < HEAD_DIM
    factor = HEAD_DIM**-0.5
    for sample in range(samples):
        rows = slice(sample * PATCHES, (sample + 1) * PATCHES)
        for pair in range(PAIRS):
            at = pair * LANES
            queries = packed[rows, at : at + LANES]
            keys = block_diagonal(packed[rows, D + at : D + at + LANES], first_half)
            values = block_diagonal(packed[rows, 2 * D + at : 2 * D + at + LANES], first_half)
            attend = chance[rows, at : at + LANES]
            grad_pair = grad_mixed[rows, at : at + LANES]
            grad_attend = dot(grad_pair, values, 1, 1)
            inner = spread_halves(jnp.sum, attend * grad_attend, first_half, 0.0)
            grad_scores = (attend * (grad_attend - inner)).astype(jnp.bfloat16)
            grad_queries = dot(grad_scores, keys, 1, 0) * factor
            grad_keys = dot(grad_scores, queries, 0, 0)
            grad_keys = jnp.where(first_half, grad_keys[:PATCHES], grad_keys[PATCHES:]) * factor
            grad_values = dot(attend.astype(jnp.bfloat16), grad_pair, 0, 0)
            grad_values = jnp.where(first_half, grad_values[:PATCHES], grad_values[PATCHES:])
            grad_packed[rows, at : at + LANES] = grad_queries.astype(jnp.bfloat16)
            grad_packed[rows, D + at : D + at + LANES] = grad_keys.astype(jnp.bfloat16)
            grad_packed[rows, 2 * D + at : 2 * D + at + LANES] = grad_values.astype(jnp.bfloat16)
    hat, scale = normalize(tokens[...].astype(jnp.float32))
    gain = vector(vectors, "gain_one")
    normed = (hat * gain + vector(vectors, "shift_one")).astype(jnp.bfloat16)
    acc_qkv[...] += dot(normed, grad_packed[...], 0, 0)
    grad_normed = dot(grad_packed[...], w_qkv[...], 1, 1)
    add_vector("gain_one", grad_normed * hat)
    add_vector("shift_one", grad_normed)
    grad_input[...] = (grad_through + norm_back(grad_normed, gain, hat, scale)).astype(
        jnp.bfloat16
    )

    @pl.when(step == pl.num_programs(0) - 1)
    def _():
        flatten(acc_qkv, grad_qkv, 0)
        flatten(acc_out, grad_w_out, 0)


def attention_back(tokens, packed, chance, mixed, grad_hidden, w_qkv, w_out, vectors, block):
    rows = tokens.shape[0]

    def by_rows(width):
        return pl.BlockSpec((block, width), lambda i: (i, 0))

    def whole(shape):
        return pl.BlockSpec(shape, lambda i: (0, 0))

    return pl.pallas_call(
        attention_back_kernel,
        name="attention_back",
        grid=(rows // block,),
        in_specs=[
            by_rows(D),
            by_rows(3 * D),
            by_rows(D),
            by_rows(D),
            by_rows(D),
            whole(w_qkv.shape),
            whole(w_out.shape),
            whole(vectors.shape),
        ],
        out_specs=[by_rows(D), whole((QKV_ROWS, LANES)), whole((OUT_ROWS, LANES)), whole((8, FF))],
        scratch_shapes=[
            pltpu.VMEM((D, 3 * D), jnp.float32),
            pltpu.VMEM((D, D), jnp.float32),
            pltpu.VMEM((block, 3 * D), jnp.bfloat16),
        ],
        out_shape=(
            jax.ShapeDtypeStruct((rows, D), jnp.bfloat16),
            jax.ShapeDtypeStruct((QKV_ROWS, LANES), jnp.float32),
            jax.ShapeDtypeStruct((OUT_ROWS, LANES), jnp.float32),
            jax.ShapeDtypeStruct((8, FF), jnp.float32),
        ),
        compiler_params=pltpu.CompilerParams(vmem_limit_bytes=VMEM_LIMIT),
    )(tokens, packed, chance, mixed, grad_hidden, w_qkv, w_out, vectors)


def pack_kernel(
    starts, grad_qkv, grad_out, grad_up, grad_down, vectors, kept, sent, flat
):
    half, rows, _ = kept.shape
    flat[0:QKV_ROWS, :] = grad_qkv[...]
    flat[BASE_OUT : BASE_OUT + OUT_ROWS, :] = grad_out[...]
    flat[BASE_UP : BASE_UP + UP_ROWS, :] = grad_up[...]
    flat[BASE_DOWN : BASE_DOWN + UP_ROWS, :] = grad_down[...]
    row = BASE_VEC
    for index, name in enumerate(VECTORS):
        for block in range(vector_width(name) // LANES):
            flat[row : row + 1, :] = vectors[
                index : index + 1, block * LANES : (block + 1) * LANES
            ]
            row += 1
    flat[row:, :] = jnp.zeros_like(flat[row:, :])
    for slot in range(half):
        kept[slot] = flat[pl.ds(pl.multiple_of(starts[slot], 8), rows), :]
        sent[slot] = flat[pl.ds(pl.multiple_of(starts[half + slot], 8), rows), :].astype(
            jnp.bfloat16
        )


def pack(starts, grad_qkv, grad_out, grad_up, grad_down, vectors, shard, devices):
    rows = chunk_rows(shard)
    flat_rows = max(chunk_start(devices - 1, shard) + rows, round_up(FLAT_ROWS, 8))
    inputs = (grad_qkv, grad_out, grad_up, grad_down, vectors)

    def whole(shape):
        return pl.BlockSpec(shape, lambda i, starts: (0,) * len(shape))

    shape = (devices // 2, rows, LANES)
    return pl.pallas_call(
        pack_kernel,
        name="pack",
        grid_spec=pltpu.PrefetchScalarGridSpec(
            num_scalar_prefetch=1,
            grid=(1,),
            in_specs=[whole(array.shape) for array in inputs],
            out_specs=[whole(shape), whole(shape)],
            scratch_shapes=[pltpu.VMEM((flat_rows, LANES), jnp.float32)],
        ),
        out_shape=(
            jax.ShapeDtypeStruct(shape, jnp.float32),
            jax.ShapeDtypeStruct(shape, jnp.bfloat16),
        ),
        compiler_params=pltpu.CompilerParams(vmem_limit_bytes=VMEM_LIMIT),
    )(starts, *inputs)


def step_scale(position):
    bound_one = QKV_ROWS * LANES
    bound_two = BASE_UP * LANES
    bound_three = BASE_DOWN * LANES
    bound_four = BASE_VEC * LANES
    scale = jnp.where(
        position < bound_one,
        D ** (-0.5),
        jnp.where(
            position < bound_two,
            (D // 8) ** (-0.5),
            jnp.where(
                position < bound_three,
                D ** (-0.5),
                jnp.where(position < bound_four, FF ** (-0.5), 0.1),
            ),
        ),
    )
    decay = jnp.where(position < bound_four, 0.05, 0.0)
    return (scale, decay)


def on_device(tokens, counts, cotangent, master, first, second, rate, step):
    shard = master.shape[0]
    devices = lax.axis_size(AXES)
    me = lax.axis_index(AXES)
    rows = chunk_rows(shard)
    offset = me * shard % 1024
    own = lax.dynamic_update_slice(
        jnp.zeros((rows * LANES,), jnp.bfloat16), master.astype(jnp.bfloat16), (offset,)
    ).reshape(rows, LANES)
    swaps, core_swap, owners = exchange_plan(lax.axis_size("wide"), lax.axis_size("narrow"))
    starts = jnp.asarray(chunk_start(owners, shard).astype(np.int32))[me]
    pieces = gather_chunks(own, swaps, core_swap)
    w_qkv, w_out, w_up, w_down, vectors = unpack(starts, pieces, shard)
    packed, chance, mixed, hidden = attention(counts, tokens, w_qkv, w_out, vectors, 512)
    result, grad_hidden, grad_up, grad_down, vectors_two = feed(
        counts, hidden, cotangent, w_up, w_down, vectors, 256, 512
    )
    grad_input, grad_qkv, grad_out, vectors_one = attention_back(
        tokens, packed, chance, mixed, grad_hidden, w_qkv, w_out, vectors, 512
    )
    kept, sent = pack(
        starts, grad_qkv, grad_out, grad_up, grad_down, vectors_one + vectors_two, shard, devices
    )
    reduced = scatter_chunks(kept, sent, swaps, core_swap)
    reduced = lax.dynamic_slice(
        reduced.reshape(rows * LANES), (offset,), (shard,)
    )
    position = me * shard + jnp.arange(shard, dtype=jnp.int32)
    first_new = 0.5 * first + 0.5 * reduced
    second_new = 0.5 * second + 0.5 * reduced * reduced
    correct = 1.0 - jnp.power(jnp.float32(0.5), step[0].astype(jnp.float32))
    scale, decay = step_scale(position)
    moved = first_new / correct / (jnp.sqrt(second_new / correct) + 1e-08)
    master_new = master - rate[0] * scale * (moved + decay * master)
    return (
        result,
        grad_input,
        master_new,
        first_new,
        second_new,
        master_new.astype(jnp.bfloat16),
    )


def solution(mesh):
    split = P(AXES)
    by_rows = P(AXES, None)
    return jax.shard_map(
        on_device,
        mesh=mesh,
        in_specs=(by_rows, split, by_rows, split, split, split, P(), P()),
        out_specs=(by_rows, by_rows, split, split, split, split),
        check_vma=False,
    )
```

```python
import functools
import itertools

import jax
import jax.numpy as jnp
from jax import lax
from jax.experimental import pallas as pl
from jax.experimental.pallas import tpu as pltpu
from jax.sharding import PartitionSpec as P

D = 384
FF = 1536
HEADS = 6
HEAD_DIM = 64
PATCHES = 64
LANES = 128
PAIRS = HEADS // 2
EPS = 1e-06
AXES = ("wide", "narrow")
QKV_ROWS = 3 * D * D // LANES
OUT_ROWS = D * D // LANES
UP_ROWS = D * FF // LANES
VEC_ROWS = (6 * D + FF) // LANES
FLAT_ROWS = QKV_ROWS + OUT_ROWS + 2 * UP_ROWS + VEC_ROWS
BASE_OUT = QKV_ROWS
BASE_UP = BASE_OUT + OUT_ROWS
BASE_DOWN = BASE_UP + UP_ROWS
BASE_VEC = BASE_DOWN + UP_ROWS
VECTORS = ("gain_one", "shift_one", "bias_out", "gain_two", "shift_two", "bias_up", "bias_down")
VMEM_LIMIT = 60 * 1024 * 1024
BLOCK = 512
GROUP = 8
COLUMNS = 512
FLOWS = 1


def round_up(value, step):
    return (value + step - 1) // step * step


def dot(left, right, left_dim, right_dim):
    return lax.dot_general(
        left, right, (((left_dim,), (right_dim,)), ((), ())), preferred_element_type=jnp.float32
    )


def chunk_rows(shard):
    return round_up(shard + 1024, 16 * FLOWS * LANES) // LANES


class Flow:
    def __init__(self, rounds, devices, core):
        self.swaps = [
            [(device, device ^ pair[1 if device & core else 0]) for device in range(devices)]
            for pair in rounds
        ]
        self.core_swap = [(device, device ^ core) for device in range(devices)]
        self.core = core
        half = devices // 2
        self.across = [[0] * devices, [0] * devices]
        for side in (0, 1):
            for slot in range(half):
                for index, pair in enumerate(rounds):
                    if slot >> index & 1:
                        self.across[side][slot] ^= pair[side]
                        self.across[1 - side][half + slot] ^= pair[side]
                self.across[1 - side][half + slot] ^= core

    def owner(self, me, slot):
        side_one = (me & self.core) != 0
        return me ^ jnp.where(side_one, self.across[1][slot], self.across[0][slot])


def exchange_flows(wide, narrow):
    devices = wide * narrow
    core = narrow
    bits = [1 << k for k in reversed(range(devices.bit_length() - 1)) if 1 << k != core]
    half = (len(bits) + 1) // 2
    flows = []
    for order in range(FLOWS):
        rounds = []
        for first, second in itertools.zip_longest(bits[:half], bits[half:]):
            if second is None:
                rounds.append((first, first))
            else:
                rounds += [(first, second), (second, first)]
        flows.append(Flow(rounds, devices, core))
    return flows


def gather_chunks(own, flow):
    held = own[None]
    for swap in flow.swaps[:-1]:
        held = jnp.concatenate([held, lax.ppermute(held, AXES, swap)], axis=0)
    held_core = lax.ppermute(held, AXES, flow.core_swap)
    taken = lax.ppermute(held, AXES, flow.swaps[-1])
    taken_core = lax.ppermute(taken, AXES, flow.core_swap)
    return held, taken, held_core, taken_core


def scatter_chunks(kept, sent, flow):
    parts = [kept, lax.ppermute(sent, AXES, flow.core_swap)]
    for swap in reversed(flow.swaps):
        half = parts[0].shape[0] // 2
        upper = sum(part[half:].astype(jnp.float32) for part in parts)
        parts = [part[:half] for part in parts]
        parts.append(lax.ppermute(upper.astype(jnp.bfloat16), AXES, swap))
    return sum(part[0].astype(jnp.float32) for part in parts)


def vector_width(name):
    return FF if name == "bias_up" else D


def vector_rows():
    row = BASE_VEC
    for index, name in enumerate(VECTORS):
        for block in range(vector_width(name) // LANES):
            yield index, slice(block * LANES, (block + 1) * LANES), row
            row += 1


def matrix_blocks(matrix, base):
    height, width = matrix.shape
    blocks = width // LANES
    for block in range(blocks):
        columns = slice(block * LANES, (block + 1) * LANES)
        yield columns, pl.ds(base + block, height, stride=blocks)


def first_row(owner, shard):
    return owner * shard // 1024 * 8


def dynamic_first_row(owner, shard):
    return pl.multiple_of(lax.shift_right_logical(owner * shard, 10) * 8, 8)


def unpack(me, pieces, flows, shard, flat, w_qkv, w_out, w_up, w_down, vectors):
    rows = pieces[0].shape[1]
    devices = 4 * pieces[0].shape[0]
    sure = shard // 1024 * 8
    for owner in range(devices):
        start = first_row(owner, shard)
        flat[start : start + 8, :] = jnp.zeros((8, LANES), jnp.float32)
        flat[start + sure : start + FLOWS * rows, :] = jnp.zeros(
            (FLOWS * rows - sure, LANES), jnp.float32
        )
    for index, flow in enumerate(flows):
        low, high = index * rows, (index + 1) * rows
        cuts = sorted({low, high} | {cut for cut in (8, sure) if low < cut < high})
        for slot in range(devices):
            source = pieces[4 * index + slot * 4 // devices]
            start = dynamic_first_row(flow.owner(me, slot), shard)
            for begin, end in zip(cuts, cuts[1:]):
                piece = source[slot % source.shape[0], begin - low : end - low, :]
                piece = piece.astype(jnp.float32)
                target = (pl.ds(pl.multiple_of(start + begin, 8), end - begin), slice(None))
                if begin < 8 or begin >= sure:
                    flat[target] += piece
                else:
                    flat[target] = piece
    for matrix, base in ((w_qkv, 0), (w_out, BASE_OUT), (w_up, BASE_UP), (w_down, BASE_DOWN)):
        for columns, rows_of in matrix_blocks(matrix, base):
            matrix[:, columns] = flat[rows_of, :].astype(jnp.bfloat16)
    for index, columns, row in vector_rows():
        vectors[index : index + 1, columns] = flat[row : row + 1, :]


def pack(me, flows, shard, flat, grad_qkv, grad_out, grad_up, grad_down, vectors, outputs):
    for matrix, base in (
        (grad_qkv, 0),
        (grad_out, BASE_OUT),
        (grad_up, BASE_UP),
        (grad_down, BASE_DOWN),
    ):
        for columns, rows_of in matrix_blocks(matrix, base):
            flat[rows_of, :] = matrix[:, columns]
    for index, columns, row in vector_rows():
        flat[row : row + 1, :] = vectors[index : index + 1, columns]
    flat[FLAT_ROWS:, :] = jnp.zeros((flat.shape[0] - FLAT_ROWS, LANES), jnp.float32)
    for index, flow in enumerate(flows):
        kept, sent = outputs[2 * index : 2 * index + 2]
        half, rows, _ = kept.shape
        for slot in range(half):
            start = dynamic_first_row(flow.owner(me, slot), shard) + index * rows
            kept[slot] = flat[pl.ds(pl.multiple_of(start, 8), rows), :]
            start = dynamic_first_row(flow.owner(me, half + slot), shard) + index * rows
            sent[slot] = flat[pl.ds(pl.multiple_of(start, 8), rows), :].astype(jnp.bfloat16)


def vector(vectors, name):
    index = VECTORS.index(name)
    return vectors[index : index + 1, : vector_width(name)]


def normalize(values):
    center = values - jnp.mean(values, axis=-1, keepdims=True)
    spread = jnp.mean(center * center, axis=-1, keepdims=True)
    scale = lax.rsqrt(spread + EPS)
    return center * scale, scale


def norm_back(grad, gain, hat, scale):
    inner = grad * gain
    mean_inner = jnp.mean(inner, axis=-1, keepdims=True)
    mean_cross = jnp.mean(inner * hat, axis=-1, keepdims=True)
    return scale * (inner - mean_inner - hat * mean_cross)


def first_halves():
    return lax.broadcasted_iota(jnp.int32, (PATCHES, LANES), 1) < HEAD_DIM


def block_diagonal(values, first_half):
    zero = jnp.zeros_like(values)
    return jnp.concatenate(
        [jnp.where(first_half, values, zero), jnp.where(first_half, zero, values)], axis=0
    )


def own_halves(values, first_half):
    return jnp.where(first_half, values[:PATCHES], values[PATCHES:])


def head_chains(samples):
    for sample in range(0, samples, GROUP):
        yield [
            (slice(each * PATCHES, (each + 1) * PATCHES), pair * LANES, each)
            for each in range(sample, min(sample + GROUP, samples))
            for pair in range(PAIRS)
        ]


def attention(count, packed, chance, mixed):
    first_half = first_halves()
    slots = lax.broadcasted_iota(jnp.int32, (PATCHES, LANES), 0)
    for chains in head_chains(packed.shape[0] // PATCHES):
        scores = [
            dot(
                packed[rows, D + at : D + at + LANES],
                block_diagonal(packed[rows, at : at + LANES], first_half),
                1,
                1,
            )
            for rows, at, _ in chains
        ]
        scores = [
            jnp.where(slots < count(each), score * HEAD_DIM**-0.5, -1e30)
            for score, (_, _, each) in zip(scores, chains)
        ]
        exponents = [jnp.exp(score - jnp.max(score, axis=0, keepdims=True)) for score in scores]
        attends = [
            exponent * (1.0 / jnp.sum(exponent, axis=0, keepdims=True)) for exponent in exponents
        ]
        for attend, (rows, at, _) in zip(attends, chains):
            chance[rows, at : at + LANES] = attend
        mixes = [
            dot(attend.astype(jnp.bfloat16), packed[rows, 2 * D + at : 2 * D + at + LANES], 0, 0)
            for attend, (rows, at, _) in zip(attends, chains)
        ]
        for mix, (rows, at, _) in zip(mixes, chains):
            mixed[rows, at : at + LANES] = own_halves(mix, first_half).astype(jnp.bfloat16)


def attention_back(packed, chance, grad_mixed, grad_packed):
    first_half = first_halves()
    factor = HEAD_DIM**-0.5
    for chains in head_chains(packed.shape[0] // PATCHES):
        sides = [
            block_diagonal(grad_mixed[rows, at : at + LANES], first_half) for rows, at, _ in chains
        ]
        grad_attends = [
            dot(packed[rows, 2 * D + at : 2 * D + at + LANES], side, 1, 1)
            for side, (rows, at, _) in zip(sides, chains)
        ]
        attends = [chance[rows, at : at + LANES] for rows, at, _ in chains]
        grad_values = [
            dot(attend.astype(jnp.bfloat16), side, 1, 0) for attend, side in zip(attends, sides)
        ]
        for grad, (rows, at, _) in zip(grad_values, chains):
            grad_packed[rows, 2 * D + at : 2 * D + at + LANES] = grad.astype(jnp.bfloat16)
        inners = [
            jnp.sum(attend * grad, axis=0, keepdims=True)
            for attend, grad in zip(attends, grad_attends)
        ]
        grad_scores = [
            (attend * (grad - inner)).astype(jnp.bfloat16)
            for attend, grad, inner in zip(attends, grad_attends, inners)
        ]
        grad_keys = [
            dot(grad, block_diagonal(packed[rows, at : at + LANES], first_half), 1, 0) * factor
            for grad, (rows, at, _) in zip(grad_scores, chains)
        ]
        for grad, (rows, at, _) in zip(grad_keys, chains):
            grad_packed[rows, D + at : D + at + LANES] = grad.astype(jnp.bfloat16)
        grad_queries = [
            dot(grad, packed[rows, D + at : D + at + LANES], 0, 0)
            for grad, (rows, at, _) in zip(grad_scores, chains)
        ]
        for grad, (rows, at, _) in zip(grad_queries, chains):
            grad_packed[rows, at : at + LANES] = (own_halves(grad, first_half) * factor).astype(
                jnp.bfloat16
            )


def layer_kernel(flows, shard, *refs):
    me, counts = refs[:2]
    pieces = refs[2 : 2 + 4 * FLOWS]
    tokens, cotangent, result, grad_input = refs[2 + 4 * FLOWS : 6 + 4 * FLOWS]
    outputs = refs[6 + 4 * FLOWS : 6 + 6 * FLOWS]
    (
        flat,
        w_qkv,
        w_out,
        w_up,
        w_down,
        vectors,
        acc_qkv,
        acc_out,
        acc_up,
        acc_down,
        acc_vectors,
        packed,
        chance,
        mixed,
        grad_mixed,
        grad_packed,
    ) = refs[6 + 6 * FLOWS :]
    step = pl.program_id(0)
    samples = tokens.shape[0] // PATCHES

    @pl.when(step == 0)
    def _():
        unpack(me[0], pieces, flows, shard, flat, w_qkv, w_out, w_up, w_down, vectors)
        for ref in (acc_qkv, acc_out, acc_up, acc_down, acc_vectors):
            ref[...] = jnp.zeros_like(ref)

    def count(sample):
        return counts[step * samples + sample]

    def add_vector(name, values, at=0):
        index = VECTORS.index(name)
        acc_vectors[index : index + 1, at : at + values.shape[1]] += jnp.sum(
            values, axis=0, keepdims=True
        )

    inputs = tokens[...].astype(jnp.float32)
    hat_one, scale_one = normalize(inputs)
    gain_one = vector(vectors, "gain_one")
    normed_one = (hat_one * gain_one + vector(vectors, "shift_one")).astype(jnp.bfloat16)
    packed[...] = dot(normed_one, w_qkv[...], 1, 0).astype(jnp.bfloat16)
    attention(count, packed, chance, mixed)
    hidden = inputs + dot(mixed[...], w_out[...], 1, 0) + vector(vectors, "bias_out")

    hat_two, scale_two = normalize(hidden)
    gain_two = vector(vectors, "gain_two")
    normed_two = (hat_two * gain_two + vector(vectors, "shift_two")).astype(jnp.bfloat16)
    slots = lax.broadcasted_iota(jnp.int32, (PATCHES, 1), 0)
    visible = jnp.concatenate(
        [jnp.where(slots < count(sample), 1.0, 0.0) for sample in range(samples)], axis=0
    )
    grad_out = cotangent[...].astype(jnp.float32) * visible
    grad_out_low = grad_out.astype(jnp.bfloat16)
    add_vector("bias_down", grad_out)
    total = hidden + vector(vectors, "bias_down")
    grad_normed_two = jnp.zeros_like(hidden)
    bias_up = vector(vectors, "bias_up")
    for at in range(0, FF, COLUMNS):
        columns = slice(at, at + COLUMNS)
        upward = dot(normed_two, w_up[:, columns], 1, 0) + bias_up[:, columns]
        below = 0.5 * (1.0 + lax.erf(upward * 0.5**0.5))
        active = (upward * below).astype(jnp.bfloat16)
        slope = below + upward * (jnp.exp(-0.5 * upward * upward) * (0.5 / jnp.pi) ** 0.5)
        total = total + dot(active, w_down[columns, :], 1, 0)
        grad_upward = dot(grad_out_low, w_down[columns, :], 1, 1) * slope
        grad_upward = grad_upward.astype(jnp.bfloat16)
        add_vector("bias_up", grad_upward.astype(jnp.float32), at)
        acc_down[columns, :] += dot(active, grad_out_low, 0, 0)
        acc_up[:, columns] += dot(normed_two, grad_upward, 0, 0)
        grad_normed_two = grad_normed_two + dot(grad_upward, w_up[:, columns], 1, 1)
    result[...] = total.astype(jnp.bfloat16)
    add_vector("gain_two", grad_normed_two * hat_two)
    add_vector("shift_two", grad_normed_two)
    grad_hidden = grad_out + norm_back(grad_normed_two, gain_two, hat_two, scale_two)

    grad_hidden_low = grad_hidden.astype(jnp.bfloat16)
    add_vector("bias_out", grad_hidden_low.astype(jnp.float32))
    acc_out[...] += dot(mixed[...], grad_hidden_low, 0, 0)
    grad_mixed[...] = dot(grad_hidden_low, w_out[...], 1, 1).astype(jnp.bfloat16)
    attention_back(packed, chance, grad_mixed, grad_packed)
    acc_qkv[...] += dot(normed_one, grad_packed[...], 0, 0)
    grad_normed_one = dot(grad_packed[...], w_qkv[...], 1, 1)
    add_vector("gain_one", grad_normed_one * hat_one)
    add_vector("shift_one", grad_normed_one)
    grad_input[...] = (
        grad_hidden + norm_back(grad_normed_one, gain_one, hat_one, scale_one)
    ).astype(jnp.bfloat16)

    @pl.when(step == pl.num_programs(0) - 1)
    def _():
        pack(
            me[0], flows, shard, flat, acc_qkv, acc_out, acc_up, acc_down, acc_vectors, outputs
        )


def layer(me, counts, pieces, tokens, cotangent, flows, shard):
    rows = tokens.shape[0]
    block = min(BLOCK, rows)
    quarter, piece_rows, _ = pieces[0].shape
    devices = 4 * quarter
    flat_rows = first_row(devices - 1, shard) + FLOWS * piece_rows
    low = jnp.bfloat16
    full = jnp.float32

    def by_rows():
        return pl.BlockSpec((block, D), lambda i, me, counts: (i, 0))

    def whole(shape):
        return pl.BlockSpec(
            shape, lambda i, me, counts: (0,) * len(shape), pipeline_mode=pl.Buffered(1)
        )

    chunk_shape = (devices // 2, piece_rows, LANES)
    return pl.pallas_call(
        functools.partial(layer_kernel, flows, shard),
        name="layer",
        grid_spec=pltpu.PrefetchScalarGridSpec(
            num_scalar_prefetch=2,
            grid=(rows // block,),
            in_specs=[whole(piece.shape) for piece in pieces] + [by_rows(), by_rows()],
            out_specs=[by_rows(), by_rows()] + [whole(chunk_shape)] * (2 * FLOWS),
            scratch_shapes=[
                pltpu.VMEM((flat_rows, LANES), full),
                pltpu.VMEM((D, 3 * D), low),
                pltpu.VMEM((D, D), low),
                pltpu.VMEM((D, FF), low),
                pltpu.VMEM((FF, D), low),
                pltpu.VMEM((8, FF), full),
                pltpu.VMEM((D, 3 * D), full),
                pltpu.VMEM((D, D), full),
                pltpu.VMEM((D, FF), full),
                pltpu.VMEM((FF, D), full),
                pltpu.VMEM((8, FF), full),
                pltpu.VMEM((block, 3 * D), low),
                pltpu.VMEM((block, D), full),
                pltpu.VMEM((block, D), low),
                pltpu.VMEM((block, D), low),
                pltpu.VMEM((block, 3 * D), low),
            ],
        ),
        out_shape=[jax.ShapeDtypeStruct((rows, D), low)] * 2
        + [jax.ShapeDtypeStruct(chunk_shape, dtype) for dtype in (full, low)] * FLOWS,
        compiler_params=pltpu.CompilerParams(vmem_limit_bytes=VMEM_LIMIT),
    )(me, counts, *pieces, tokens, cotangent)


def step_scale(position):
    bound_one = QKV_ROWS * LANES
    bound_two = BASE_UP * LANES
    bound_three = BASE_DOWN * LANES
    bound_four = BASE_VEC * LANES
    scale = jnp.where(
        position < bound_one,
        D ** (-0.5),
        jnp.where(
            position < bound_two,
            (D // 8) ** (-0.5),
            jnp.where(
                position < bound_three,
                D ** (-0.5),
                jnp.where(position < bound_four, FF ** (-0.5), 0.1),
            ),
        ),
    )
    decay = jnp.where(position < bound_four, 0.05, 0.0)
    return (scale, decay)


def on_device(tokens, counts, cotangent, master, first, second, rate, step):
    shard = master.shape[0]
    me = lax.axis_index(AXES)
    flows = exchange_flows(lax.axis_size("wide"), lax.axis_size("narrow"))
    rows = chunk_rows(shard)
    offset = me * shard % 1024
    own = lax.dynamic_update_slice(
        jnp.zeros((rows * LANES,), jnp.bfloat16), master.astype(jnp.bfloat16), (offset,)
    ).reshape(FLOWS, rows // FLOWS, LANES)
    pieces = []
    for index, flow in enumerate(flows):
        pieces += gather_chunks(own[index], flow)
    result, grad_input, *chunks = layer(
        me.reshape(1), counts, pieces, tokens, cotangent, flows, shard
    )
    reduced = jnp.concatenate(
        [
            scatter_chunks(chunks[2 * index], chunks[2 * index + 1], flow)
            for index, flow in enumerate(flows)
        ],
        axis=0,
    )
    reduced = lax.dynamic_slice(reduced.reshape(rows * LANES), (offset,), (shard,))
    position = me * shard + jnp.arange(shard, dtype=jnp.int32)
    first_new = 0.5 * first + 0.5 * reduced
    second_new = 0.5 * second + 0.5 * reduced * reduced
    correct = 1.0 - jnp.power(jnp.float32(0.5), step[0].astype(jnp.float32))
    scale, decay = step_scale(position)
    moved = first_new / correct / (jnp.sqrt(second_new / correct) + 1e-08)
    master_new = master - rate[0] * scale * (moved + decay * master)
    return (
        result,
        grad_input,
        master_new,
        first_new,
        second_new,
        master_new.astype(jnp.bfloat16),
    )


def solution(mesh):
    split = P(AXES)
    by_rows = P(AXES, None)
    return jax.shard_map(
        on_device,
        mesh=mesh,
        in_specs=(by_rows, split, by_rows, split, split, split, P(), P()),
        out_specs=(by_rows, by_rows, split, split, split, split),
        check_vma=False,
    )
```

```python
import functools

import jax
import jax.numpy as jnp
from jax import lax
from jax.experimental import pallas as pl
from jax.experimental.pallas import tpu as pltpu
from jax.sharding import PartitionSpec as P

D = 384
FF = 1536
HEADS = 6
HEAD_DIM = 64
PATCHES = 64
LANES = 128
PAIRS = HEADS // 2
EPS = 1e-06
AXES = ("wide", "narrow")
QKV_ROWS = 3 * D * D // LANES
OUT_ROWS = D * D // LANES
UP_ROWS = D * FF // LANES
VEC_ROWS = (6 * D + FF) // LANES
FLAT_ROWS = QKV_ROWS + OUT_ROWS + 2 * UP_ROWS + VEC_ROWS
BASE_OUT = QKV_ROWS
BASE_UP = BASE_OUT + OUT_ROWS
BASE_DOWN = BASE_UP + UP_ROWS
BASE_VEC = BASE_DOWN + UP_ROWS
VECTORS = ("gain_one", "shift_one", "bias_out", "gain_two", "shift_two", "bias_up", "bias_down")
VMEM_LIMIT = 60 * 1024 * 1024
BLOCK = 512
GROUP = 8
COLUMNS = 512
FLOWS = 2


def round_up(value, step):
    return (value + step - 1) // step * step


def dot(left, right, left_dim, right_dim):
    return lax.dot_general(
        left, right, (((left_dim,), (right_dim,)), ((), ())), preferred_element_type=jnp.float32
    )


def chunk_rows(shard):
    return round_up(shard + 1024, 16 * FLOWS * LANES) // LANES


class Flow:
    def __init__(self, rounds, devices, core):
        self.swaps = [
            [(device, device ^ pair[1 if device & core else 0]) for device in range(devices)]
            for pair in rounds
        ]
        self.core_swap = [(device, device ^ core) for device in range(devices)]
        self.core = core
        half = devices // 2
        self.across = [[0] * devices, [0] * devices]
        for side in (0, 1):
            for slot in range(half):
                for index, pair in enumerate(rounds):
                    if slot >> index & 1:
                        self.across[side][slot] ^= pair[side]
                        self.across[1 - side][half + slot] ^= pair[side]
                self.across[1 - side][half + slot] ^= core

    def owner(self, me, slot):
        side_one = (me & self.core) != 0
        return me ^ jnp.where(side_one, self.across[1][slot], self.across[0][slot])


def gather_flows(wide, narrow):
    bits = chip_bits(wide * narrow, narrow)
    upper, (first, second) = bits[:-2], bits[-2:]
    orders = [
        (upper + [first, second], upper + [second, first]),
        (
            [first] + upper[:-1] + [second] + upper[-1:],
            [second] + upper[:-1] + [first] + upper[-1:],
        ),
    ]
    return [Flow(list(zip(*order)), wide * narrow, narrow) for order in orders]


def scatter_flows(wide, narrow):
    bits = chip_bits(wide * narrow, narrow)
    upper, (first, second) = bits[:-2], bits[-2:]
    orders = [
        (upper + [first, second], upper + [second, first]),
        ([first] + upper + [second], [second] + upper + [first]),
    ]
    return [Flow(list(zip(*order)), wide * narrow, narrow) for order in orders]


def chip_bits(devices, core):
    return [1 << k for k in reversed(range(devices.bit_length() - 1)) if 1 << k != core]


def gather_chunks(own, flow):
    held = own[None]
    for swap in flow.swaps[:-1]:
        held = jnp.concatenate([held, lax.ppermute(held, AXES, swap)], axis=0)
    held_core = lax.ppermute(held, AXES, flow.core_swap)
    taken = lax.ppermute(held, AXES, flow.swaps[-1])
    taken_core = lax.ppermute(taken, AXES, flow.core_swap)
    return held, taken, held_core, taken_core


def scatter_chunks(kept, sent, flow):
    parts = [kept, lax.ppermute(sent, AXES, flow.core_swap)]
    for swap in reversed(flow.swaps):
        half = parts[0].shape[0] // 2
        upper = sum(part[half:].astype(jnp.float32) for part in parts)
        parts = [part[:half] for part in parts]
        parts.append(lax.ppermute(upper.astype(jnp.bfloat16), AXES, swap))
    return sum(part[0].astype(jnp.float32) for part in parts)


def vector_width(name):
    return FF if name == "bias_up" else D


def vector_rows():
    row = BASE_VEC
    for index, name in enumerate(VECTORS):
        for block in range(vector_width(name) // LANES):
            yield index, slice(block * LANES, (block + 1) * LANES), row
            row += 1


def matrix_blocks(matrix, base):
    height, width = matrix.shape
    blocks = width // LANES
    for block in range(blocks):
        columns = slice(block * LANES, (block + 1) * LANES)
        yield columns, pl.ds(base + block, height, stride=blocks)


def first_row(owner, shard):
    return owner * shard // 1024 * 8


def dynamic_first_row(owner, shard):
    return pl.multiple_of(lax.shift_right_logical(owner * shard, 10) * 8, 8)


def unpack(me, pieces, flows, shard, flat, w_qkv, w_out, w_up, w_down, vectors):
    rows = pieces[0].shape[1]
    devices = 4 * pieces[0].shape[0]
    sure = shard // 1024 * 8
    for owner in range(devices):
        start = first_row(owner, shard)
        flat[start : start + 8, :] = jnp.zeros((8, LANES), jnp.float32)
        flat[start + sure : start + FLOWS * rows, :] = jnp.zeros(
            (FLOWS * rows - sure, LANES), jnp.float32
        )
    for index, flow in enumerate(flows):
        low, high = index * rows, (index + 1) * rows
        cuts = sorted({low, high} | {cut for cut in (8, sure) if low < cut < high})
        for slot in range(devices):
            source = pieces[4 * index + slot * 4 // devices]
            start = dynamic_first_row(flow.owner(me, slot), shard)
            for begin, end in zip(cuts, cuts[1:]):
                piece = source[slot % source.shape[0], begin - low : end - low, :]
                piece = piece.astype(jnp.float32)
                target = (pl.ds(pl.multiple_of(start + begin, 8), end - begin), slice(None))
                if begin < 8 or begin >= sure:
                    flat[target] += piece
                else:
                    flat[target] = piece
    for matrix, base in ((w_qkv, 0), (w_out, BASE_OUT), (w_up, BASE_UP), (w_down, BASE_DOWN)):
        for columns, rows_of in matrix_blocks(matrix, base):
            matrix[:, columns] = flat[rows_of, :].astype(jnp.bfloat16)
    for index, columns, row in vector_rows():
        vectors[index : index + 1, columns] = flat[row : row + 1, :]


def pack(me, flows, shard, flat, grad_qkv, grad_out, grad_up, grad_down, vectors, outputs):
    for matrix, base in (
        (grad_qkv, 0),
        (grad_out, BASE_OUT),
        (grad_up, BASE_UP),
        (grad_down, BASE_DOWN),
    ):
        for columns, rows_of in matrix_blocks(matrix, base):
            flat[rows_of, :] = matrix[:, columns]
    for index, columns, row in vector_rows():
        flat[row : row + 1, :] = vectors[index : index + 1, columns]
    flat[FLAT_ROWS:, :] = jnp.zeros((flat.shape[0] - FLAT_ROWS, LANES), jnp.float32)
    for index, flow in enumerate(flows):
        kept, sent = outputs[2 * index : 2 * index + 2]
        half, rows, _ = kept.shape
        for slot in range(half):
            start = dynamic_first_row(flow.owner(me, slot), shard) + index * rows
            kept[slot] = flat[pl.ds(pl.multiple_of(start, 8), rows), :]
            start = dynamic_first_row(flow.owner(me, half + slot), shard) + index * rows
            sent[slot] = flat[pl.ds(pl.multiple_of(start, 8), rows), :].astype(jnp.bfloat16)


def vector(vectors, name):
    index = VECTORS.index(name)
    return vectors[index : index + 1, : vector_width(name)]


def normalize(values):
    center = values - jnp.mean(values, axis=-1, keepdims=True)
    spread = jnp.mean(center * center, axis=-1, keepdims=True)
    scale = lax.rsqrt(spread + EPS)
    return center * scale, scale


def norm_back(grad, gain, hat, scale):
    inner = grad * gain
    mean_inner = jnp.mean(inner, axis=-1, keepdims=True)
    mean_cross = jnp.mean(inner * hat, axis=-1, keepdims=True)
    return scale * (inner - mean_inner - hat * mean_cross)


def first_halves():
    return lax.broadcasted_iota(jnp.int32, (PATCHES, LANES), 1) < HEAD_DIM


def block_diagonal(values, first_half):
    zero = jnp.zeros_like(values)
    return jnp.concatenate(
        [jnp.where(first_half, values, zero), jnp.where(first_half, zero, values)], axis=0
    )


def own_halves(values, first_half):
    return jnp.where(first_half, values[:PATCHES], values[PATCHES:])


def head_chains(samples):
    for sample in range(0, samples, GROUP):
        yield [
            (slice(each * PATCHES, (each + 1) * PATCHES), pair * LANES, each)
            for each in range(sample, min(sample + GROUP, samples))
            for pair in range(PAIRS)
        ]


def attention(count, packed, chance, mixed):
    first_half = first_halves()
    slots = lax.broadcasted_iota(jnp.int32, (PATCHES, LANES), 0)
    for chains in head_chains(packed.shape[0] // PATCHES):
        scores = [
            dot(
                packed[rows, D + at : D + at + LANES],
                block_diagonal(packed[rows, at : at + LANES], first_half),
                1,
                1,
            )
            for rows, at, _ in chains
        ]
        scores = [
            jnp.where(slots < count(each), score * HEAD_DIM**-0.5, -1e30)
            for score, (_, _, each) in zip(scores, chains)
        ]
        exponents = [jnp.exp(score - jnp.max(score, axis=0, keepdims=True)) for score in scores]
        attends = [
            exponent * (1.0 / jnp.sum(exponent, axis=0, keepdims=True)) for exponent in exponents
        ]
        for attend, (rows, at, _) in zip(attends, chains):
            chance[rows, at : at + LANES] = attend
        mixes = [
            dot(attend.astype(jnp.bfloat16), packed[rows, 2 * D + at : 2 * D + at + LANES], 0, 0)
            for attend, (rows, at, _) in zip(attends, chains)
        ]
        for mix, (rows, at, _) in zip(mixes, chains):
            mixed[rows, at : at + LANES] = own_halves(mix, first_half).astype(jnp.bfloat16)


def attention_back(packed, chance, grad_mixed, grad_packed):
    first_half = first_halves()
    factor = HEAD_DIM**-0.5
    for chains in head_chains(packed.shape[0] // PATCHES):
        sides = [
            block_diagonal(grad_mixed[rows, at : at + LANES], first_half) for rows, at, _ in chains
        ]
        grad_attends = [
            dot(packed[rows, 2 * D + at : 2 * D + at + LANES], side, 1, 1)
            for side, (rows, at, _) in zip(sides, chains)
        ]
        attends = [chance[rows, at : at + LANES] for rows, at, _ in chains]
        grad_values = [
            dot(attend.astype(jnp.bfloat16), side, 1, 0) for attend, side in zip(attends, sides)
        ]
        for grad, (rows, at, _) in zip(grad_values, chains):
            grad_packed[rows, 2 * D + at : 2 * D + at + LANES] = grad.astype(jnp.bfloat16)
        inners = [
            jnp.sum(attend * grad, axis=0, keepdims=True)
            for attend, grad in zip(attends, grad_attends)
        ]
        grad_scores = [
            (attend * (grad - inner)).astype(jnp.bfloat16)
            for attend, grad, inner in zip(attends, grad_attends, inners)
        ]
        grad_keys = [
            dot(grad, block_diagonal(packed[rows, at : at + LANES], first_half), 1, 0) * factor
            for grad, (rows, at, _) in zip(grad_scores, chains)
        ]
        for grad, (rows, at, _) in zip(grad_keys, chains):
            grad_packed[rows, D + at : D + at + LANES] = grad.astype(jnp.bfloat16)
        grad_queries = [
            dot(grad, packed[rows, D + at : D + at + LANES], 0, 0)
            for grad, (rows, at, _) in zip(grad_scores, chains)
        ]
        for grad, (rows, at, _) in zip(grad_queries, chains):
            grad_packed[rows, at : at + LANES] = (own_halves(grad, first_half) * factor).astype(
                jnp.bfloat16
            )


def layer_kernel(gathers, scatters, shard, *refs):
    me, counts = refs[:2]
    pieces = refs[2 : 2 + 4 * FLOWS]
    tokens, cotangent, result, grad_input = refs[2 + 4 * FLOWS : 6 + 4 * FLOWS]
    outputs = refs[6 + 4 * FLOWS : 6 + 6 * FLOWS]
    (
        flat,
        w_qkv,
        w_out,
        w_up,
        w_down,
        vectors,
        acc_qkv,
        acc_out,
        acc_up,
        acc_down,
        acc_vectors,
        packed,
        chance,
        mixed,
        grad_mixed,
        grad_packed,
    ) = refs[6 + 6 * FLOWS :]
    step = pl.program_id(0)
    samples = tokens.shape[0] // PATCHES

    @pl.when(step == 0)
    def _():
        unpack(me[0], pieces, gathers, shard, flat, w_qkv, w_out, w_up, w_down, vectors)
        for ref in (acc_qkv, acc_out, acc_up, acc_down, acc_vectors):
            ref[...] = jnp.zeros_like(ref)

    def count(sample):
        return counts[step * samples + sample]

    def add_vector(name, values, at=0):
        index = VECTORS.index(name)
        acc_vectors[index : index + 1, at : at + values.shape[1]] += jnp.sum(
            values, axis=0, keepdims=True
        )

    inputs = tokens[...].astype(jnp.float32)
    hat_one, scale_one = normalize(inputs)
    gain_one = vector(vectors, "gain_one")
    normed_one = (hat_one * gain_one + vector(vectors, "shift_one")).astype(jnp.bfloat16)
    packed[...] = dot(normed_one, w_qkv[...], 1, 0).astype(jnp.bfloat16)
    attention(count, packed, chance, mixed)
    hidden = inputs + dot(mixed[...], w_out[...], 1, 0) + vector(vectors, "bias_out")

    hat_two, scale_two = normalize(hidden)
    gain_two = vector(vectors, "gain_two")
    normed_two = (hat_two * gain_two + vector(vectors, "shift_two")).astype(jnp.bfloat16)
    slots = lax.broadcasted_iota(jnp.int32, (PATCHES, 1), 0)
    visible = jnp.concatenate(
        [jnp.where(slots < count(sample), 1.0, 0.0) for sample in range(samples)], axis=0
    )
    grad_out = cotangent[...].astype(jnp.float32) * visible
    grad_out_low = grad_out.astype(jnp.bfloat16)
    add_vector("bias_down", grad_out)
    total = hidden + vector(vectors, "bias_down")
    grad_normed_two = jnp.zeros_like(hidden)
    bias_up = vector(vectors, "bias_up")
    for at in range(0, FF, COLUMNS):
        columns = slice(at, at + COLUMNS)
        upward = dot(normed_two, w_up[:, columns], 1, 0) + bias_up[:, columns]
        below = 0.5 * (1.0 + lax.erf(upward * 0.5**0.5))
        active = (upward * below).astype(jnp.bfloat16)
        slope = below + upward * (jnp.exp(-0.5 * upward * upward) * (0.5 / jnp.pi) ** 0.5)
        total = total + dot(active, w_down[columns, :], 1, 0)
        grad_upward = dot(grad_out_low, w_down[columns, :], 1, 1) * slope
        grad_upward = grad_upward.astype(jnp.bfloat16)
        add_vector("bias_up", grad_upward.astype(jnp.float32), at)
        acc_down[columns, :] += dot(active, grad_out_low, 0, 0)
        acc_up[:, columns] += dot(normed_two, grad_upward, 0, 0)
        grad_normed_two = grad_normed_two + dot(grad_upward, w_up[:, columns], 1, 1)
    result[...] = total.astype(jnp.bfloat16)
    add_vector("gain_two", grad_normed_two * hat_two)
    add_vector("shift_two", grad_normed_two)
    grad_hidden = grad_out + norm_back(grad_normed_two, gain_two, hat_two, scale_two)

    grad_hidden_low = grad_hidden.astype(jnp.bfloat16)
    add_vector("bias_out", grad_hidden_low.astype(jnp.float32))
    acc_out[...] += dot(mixed[...], grad_hidden_low, 0, 0)
    grad_mixed[...] = dot(grad_hidden_low, w_out[...], 1, 1).astype(jnp.bfloat16)
    attention_back(packed, chance, grad_mixed, grad_packed)
    acc_qkv[...] += dot(normed_one, grad_packed[...], 0, 0)
    grad_normed_one = dot(grad_packed[...], w_qkv[...], 1, 1)
    add_vector("gain_one", grad_normed_one * hat_one)
    add_vector("shift_one", grad_normed_one)
    grad_input[...] = (
        grad_hidden + norm_back(grad_normed_one, gain_one, hat_one, scale_one)
    ).astype(jnp.bfloat16)

    @pl.when(step == pl.num_programs(0) - 1)
    def _():
        pack(
            me[0], scatters, shard, flat, acc_qkv, acc_out, acc_up, acc_down, acc_vectors, outputs
        )


def layer(me, counts, pieces, tokens, cotangent, gathers, scatters, shard):
    rows = tokens.shape[0]
    block = min(BLOCK, rows)
    quarter, piece_rows, _ = pieces[0].shape
    devices = 4 * quarter
    flat_rows = first_row(devices - 1, shard) + FLOWS * piece_rows
    low = jnp.bfloat16
    full = jnp.float32

    def by_rows():
        return pl.BlockSpec((block, D), lambda i, me, counts: (i, 0))

    def whole(shape):
        return pl.BlockSpec(
            shape, lambda i, me, counts: (0,) * len(shape), pipeline_mode=pl.Buffered(1)
        )

    chunk_shape = (devices // 2, piece_rows, LANES)
    return pl.pallas_call(
        functools.partial(layer_kernel, gathers, scatters, shard),
        name="layer",
        grid_spec=pltpu.PrefetchScalarGridSpec(
            num_scalar_prefetch=2,
            grid=(rows // block,),
            in_specs=[whole(piece.shape) for piece in pieces] + [by_rows(), by_rows()],
            out_specs=[by_rows(), by_rows()] + [whole(chunk_shape)] * (2 * FLOWS),
            scratch_shapes=[
                pltpu.VMEM((flat_rows, LANES), full),
                pltpu.VMEM((D, 3 * D), low),
                pltpu.VMEM((D, D), low),
                pltpu.VMEM((D, FF), low),
                pltpu.VMEM((FF, D), low),
                pltpu.VMEM((8, FF), full),
                pltpu.VMEM((D, 3 * D), full),
                pltpu.VMEM((D, D), full),
                pltpu.VMEM((D, FF), full),
                pltpu.VMEM((FF, D), full),
                pltpu.VMEM((8, FF), full),
                pltpu.VMEM((block, 3 * D), low),
                pltpu.VMEM((block, D), full),
                pltpu.VMEM((block, D), low),
                pltpu.VMEM((block, D), low),
                pltpu.VMEM((block, 3 * D), low),
            ],
        ),
        out_shape=[jax.ShapeDtypeStruct((rows, D), low)] * 2
        + [jax.ShapeDtypeStruct(chunk_shape, dtype) for dtype in (full, low)] * FLOWS,
        compiler_params=pltpu.CompilerParams(vmem_limit_bytes=VMEM_LIMIT),
    )(me, counts, *pieces, tokens, cotangent)


def step_scale(position):
    bound_one = QKV_ROWS * LANES
    bound_two = BASE_UP * LANES
    bound_three = BASE_DOWN * LANES
    bound_four = BASE_VEC * LANES
    scale = jnp.where(
        position < bound_one,
        D ** (-0.5),
        jnp.where(
            position < bound_two,
            (D // 8) ** (-0.5),
            jnp.where(
                position < bound_three,
                D ** (-0.5),
                jnp.where(position < bound_four, FF ** (-0.5), 0.1),
            ),
        ),
    )
    decay = jnp.where(position < bound_four, 0.05, 0.0)
    return (scale, decay)


def on_device(tokens, counts, cotangent, master, first, second, rate, step):
    shard = master.shape[0]
    me = lax.axis_index(AXES)
    sizes = (lax.axis_size("wide"), lax.axis_size("narrow"))
    gathers, scatters = gather_flows(*sizes), scatter_flows(*sizes)
    rows = chunk_rows(shard)
    offset = me * shard % 1024
    own = lax.dynamic_update_slice(
        jnp.zeros((rows * LANES,), jnp.bfloat16), master.astype(jnp.bfloat16), (offset,)
    ).reshape(FLOWS, rows // FLOWS, LANES)
    pieces = []
    for index, flow in enumerate(gathers):
        pieces += gather_chunks(own[index], flow)
    result, grad_input, *chunks = layer(
        me.reshape(1), counts, pieces, tokens, cotangent, gathers, scatters, shard
    )
    reduced = jnp.concatenate(
        [
            scatter_chunks(chunks[2 * index], chunks[2 * index + 1], flow)
            for index, flow in enumerate(scatters)
        ],
        axis=0,
    )
    reduced = lax.dynamic_slice(reduced.reshape(rows * LANES), (offset,), (shard,))
    position = me * shard + jnp.arange(shard, dtype=jnp.int32)
    first_new = 0.5 * first + 0.5 * reduced
    second_new = 0.5 * second + 0.5 * reduced * reduced
    correct = 1.0 - jnp.power(jnp.float32(0.5), step[0].astype(jnp.float32))
    scale, decay = step_scale(position)
    moved = first_new / correct / (jnp.sqrt(second_new / correct) + 1e-08)
    master_new = master - rate[0] * scale * (moved + decay * master)
    return (
        result,
        grad_input,
        master_new,
        first_new,
        second_new,
        master_new.astype(jnp.bfloat16),
    )


def solution(mesh):
    split = P(AXES)
    by_rows = P(AXES, None)
    return jax.shard_map(
        on_device,
        mesh=mesh,
        in_specs=(by_rows, split, by_rows, split, split, split, P(), P()),
        out_specs=(by_rows, by_rows, split, split, split, split),
        check_vma=False,
    )
```

```python
import functools

import jax
import jax.numpy as jnp
from jax import lax
from jax.experimental import pallas as pl
from jax.experimental.pallas import tpu as pltpu
from jax.sharding import PartitionSpec as P

D = 384
FF = 1536
HEADS = 6
HEAD_DIM = 64
PATCHES = 64
LANES = 128
PAIRS = HEADS // 2
EPS = 1e-06
AXES = ("wide", "narrow")
QKV_ROWS = 3 * D * D // LANES
OUT_ROWS = D * D // LANES
UP_ROWS = D * FF // LANES
VEC_ROWS = (6 * D + FF) // LANES
FLAT_ROWS = QKV_ROWS + OUT_ROWS + 2 * UP_ROWS + VEC_ROWS
BASE_OUT = QKV_ROWS
BASE_UP = BASE_OUT + OUT_ROWS
BASE_DOWN = BASE_UP + UP_ROWS
BASE_VEC = BASE_DOWN + UP_ROWS
VECTORS = ("gain_one", "shift_one", "bias_out", "gain_two", "shift_two", "bias_up", "bias_down")
VMEM_LIMIT = 44 * 1024 * 1024
BLOCK = 512
GROUP = 8
COLUMNS = 512
FLOWS = 2


def round_up(value, step):
    return (value + step - 1) // step * step


def dot(left, right, left_dim, right_dim):
    return lax.dot_general(
        left, right, (((left_dim,), (right_dim,)), ((), ())), preferred_element_type=jnp.float32
    )


def chunk_rows(shard):
    return round_up(shard + 1024, 16 * FLOWS * LANES) // LANES


class Flow:
    def __init__(self, rounds, devices, core):
        self.swaps = [
            [(device, device ^ pair[1 if device & core else 0]) for device in range(devices)]
            for pair in rounds
        ]
        self.core_swap = [(device, device ^ core) for device in range(devices)]
        self.core = core
        half = devices // 2
        self.across = [[0] * devices, [0] * devices]
        for side in (0, 1):
            for slot in range(half):
                for index, pair in enumerate(rounds):
                    if slot >> index & 1:
                        self.across[side][slot] ^= pair[side]
                        self.across[1 - side][half + slot] ^= pair[side]
                self.across[1 - side][half + slot] ^= core

    def owner(self, me, slot):
        side_one = (me & self.core) != 0
        return me ^ jnp.where(side_one, self.across[1][slot], self.across[0][slot])


def exchange_flows(wide, narrow):
    bits = chip_bits(wide * narrow, narrow)
    upper, (first, second) = bits[:-2], bits[-2:]
    orders = [
        (upper + [first, second], upper + [second, first]),
        (
            upper[:1] + [second, first] + upper[1:],
            upper[:1] + [first, second] + upper[1:],
        ),
    ]
    return [Flow(list(zip(*order)), wide * narrow, narrow) for order in orders]


def chip_bits(devices, core):
    return [1 << k for k in reversed(range(devices.bit_length() - 1)) if 1 << k != core]


def after(value, other):
    if other is None:
        return value
    return lax.optimization_barrier((value, other))[0]


def gather_chunks(owns, flows):
    held = [own[None] for own in owns]
    taken = [None] * len(flows)
    turns = list(reversed(range(len(flows))))
    last = None
    for index in range(len(flows[0].swaps)):
        for turn in turns:
            if index:
                held[turn] = jnp.concatenate([after(held[turn], last), taken[turn]], axis=0)
            last = held[turn]
            taken[turn] = lax.ppermute(last, AXES, flows[turn].swaps[index])
    pieces = []
    for flow, kept, new in zip(flows, held, taken):
        pieces += [kept, new]
        pieces += [lax.ppermute(piece, AXES, flow.core_swap) for piece in (kept, new)]
    return pieces


def scatter_chunks(chunks, flows):
    parts = [
        [kept, lax.ppermute(sent, AXES, flow.core_swap)]
        for kept, sent, flow in zip(chunks[::2], chunks[1::2], flows)
    ]
    last = None
    for index in reversed(range(len(flows[0].swaps))):
        for turn, flow in enumerate(flows):
            half = parts[turn][0].shape[0] // 2
            parts[turn][0] = after(parts[turn][0], last)
            upper = sum(part[half:].astype(jnp.float32) for part in parts[turn])
            last = upper.astype(jnp.bfloat16)
            parts[turn] = [part[:half] for part in parts[turn]]
            parts[turn].append(lax.ppermute(last, AXES, flow.swaps[index]))
    return [sum(part[0].astype(jnp.float32) for part in flow) for flow in parts]


def vector_width(name):
    return FF if name == "bias_up" else D


def vector_rows():
    row = BASE_VEC
    for index, name in enumerate(VECTORS):
        for block in range(vector_width(name) // LANES):
            yield index, slice(block * LANES, (block + 1) * LANES), row
            row += 1


def matrix_blocks(matrix, base):
    height, width = matrix.shape
    blocks = width // LANES
    for block in range(blocks):
        columns = slice(block * LANES, (block + 1) * LANES)
        yield columns, pl.ds(base + block, height, stride=blocks)


def first_row(owner, shard):
    return owner * shard // 1024 * 8


def dynamic_first_row(owner, shard):
    return pl.multiple_of(lax.shift_right_logical(owner * shard, 10) * 8, 8)


def unpack(me, pieces, flows, shard, flat, w_qkv, w_out, w_up, w_down, vectors):
    rows = pieces[0].shape[1]
    devices = 4 * pieces[0].shape[0]
    sure = shard // 1024 * 8
    for owner in range(devices):
        start = first_row(owner, shard)
        flat[start : start + 8, :] = jnp.zeros((8, LANES), jnp.float32)
        flat[start + sure : start + FLOWS * rows, :] = jnp.zeros(
            (FLOWS * rows - sure, LANES), jnp.float32
        )
    for index, flow in enumerate(flows):
        low, high = index * rows, (index + 1) * rows
        cuts = sorted({low, high} | {cut for cut in (8, sure) if low < cut < high})
        for slot in range(devices):
            source = pieces[4 * index + slot * 4 // devices]
            start = dynamic_first_row(flow.owner(me, slot), shard)
            for begin, end in zip(cuts, cuts[1:]):
                piece = source[slot % source.shape[0], begin - low : end - low, :]
                piece = piece.astype(jnp.float32)
                target = (pl.ds(pl.multiple_of(start + begin, 8), end - begin), slice(None))
                if begin < 8 or begin >= sure:
                    flat[target] += piece
                else:
                    flat[target] = piece
    for matrix, base in ((w_qkv, 0), (w_out, BASE_OUT), (w_up, BASE_UP), (w_down, BASE_DOWN)):
        for columns, rows_of in matrix_blocks(matrix, base):
            matrix[:, columns] = flat[rows_of, :].astype(jnp.bfloat16)
    for index, columns, row in vector_rows():
        vectors[index : index + 1, columns] = flat[row : row + 1, :]


def pack(me, flows, shard, flat, grad_qkv, grad_out, grad_up, grad_down, vectors, outputs):
    for matrix, base in (
        (grad_qkv, 0),
        (grad_out, BASE_OUT),
        (grad_up, BASE_UP),
        (grad_down, BASE_DOWN),
    ):
        for columns, rows_of in matrix_blocks(matrix, base):
            flat[rows_of, :] = matrix[:, columns]
    for index, columns, row in vector_rows():
        flat[row : row + 1, :] = vectors[index : index + 1, columns]
    flat[FLAT_ROWS:, :] = jnp.zeros((flat.shape[0] - FLAT_ROWS, LANES), jnp.float32)
    for index, flow in enumerate(flows):
        kept, sent = outputs[2 * index : 2 * index + 2]
        half, rows, _ = kept.shape
        for slot in range(half):
            start = dynamic_first_row(flow.owner(me, slot), shard) + index * rows
            kept[slot] = flat[pl.ds(pl.multiple_of(start, 8), rows), :]
            start = dynamic_first_row(flow.owner(me, half + slot), shard) + index * rows
            sent[slot] = flat[pl.ds(pl.multiple_of(start, 8), rows), :].astype(jnp.bfloat16)


def vector(vectors, name):
    index = VECTORS.index(name)
    return vectors[index : index + 1, : vector_width(name)]


def normalize(values):
    center = values - jnp.mean(values, axis=-1, keepdims=True)
    spread = jnp.mean(center * center, axis=-1, keepdims=True)
    scale = lax.rsqrt(spread + EPS)
    return center * scale, scale


def norm_back(grad, gain, hat, scale):
    inner = grad * gain
    mean_inner = jnp.mean(inner, axis=-1, keepdims=True)
    mean_cross = jnp.mean(inner * hat, axis=-1, keepdims=True)
    return scale * (inner - mean_inner - hat * mean_cross)


def first_halves():
    return lax.broadcasted_iota(jnp.int32, (PATCHES, LANES), 1) < HEAD_DIM


def block_diagonal(values, first_half):
    zero = jnp.zeros_like(values)
    return jnp.concatenate(
        [jnp.where(first_half, values, zero), jnp.where(first_half, zero, values)], axis=0
    )


def own_halves(values, first_half):
    return jnp.where(first_half, values[:PATCHES], values[PATCHES:])


def head_chains(samples):
    for sample in range(0, samples, GROUP):
        yield [
            (slice(each * PATCHES, (each + 1) * PATCHES), pair * LANES, each)
            for each in range(sample, min(sample + GROUP, samples))
            for pair in range(PAIRS)
        ]


def attention(count, packed, chance, mixed):
    first_half = first_halves()
    slots = lax.broadcasted_iota(jnp.int32, (PATCHES, LANES), 0)
    for chains in head_chains(packed.shape[0] // PATCHES):
        scores = [
            dot(
                packed[rows, D + at : D + at + LANES],
                block_diagonal(packed[rows, at : at + LANES], first_half),
                1,
                1,
            )
            for rows, at, _ in chains
        ]
        scores = [
            jnp.where(slots < count(each), score * HEAD_DIM**-0.5, -1e30)
            for score, (_, _, each) in zip(scores, chains)
        ]
        exponents = [jnp.exp(score - jnp.max(score, axis=0, keepdims=True)) for score in scores]
        attends = [
            exponent * (1.0 / jnp.sum(exponent, axis=0, keepdims=True)) for exponent in exponents
        ]
        for attend, (rows, at, _) in zip(attends, chains):
            chance[rows, at : at + LANES] = attend
        mixes = [
            dot(attend.astype(jnp.bfloat16), packed[rows, 2 * D + at : 2 * D + at + LANES], 0, 0)
            for attend, (rows, at, _) in zip(attends, chains)
        ]
        for mix, (rows, at, _) in zip(mixes, chains):
            mixed[rows, at : at + LANES] = own_halves(mix, first_half).astype(jnp.bfloat16)


def attention_back(packed, chance, grad_mixed, grad_packed):
    first_half = first_halves()
    factor = HEAD_DIM**-0.5
    for chains in head_chains(packed.shape[0] // PATCHES):
        sides = [
            block_diagonal(grad_mixed[rows, at : at + LANES], first_half) for rows, at, _ in chains
        ]
        grad_attends = [
            dot(packed[rows, 2 * D + at : 2 * D + at + LANES], side, 1, 1)
            for side, (rows, at, _) in zip(sides, chains)
        ]
        attends = [chance[rows, at : at + LANES] for rows, at, _ in chains]
        grad_values = [
            dot(attend.astype(jnp.bfloat16), side, 1, 0) for attend, side in zip(attends, sides)
        ]
        for grad, (rows, at, _) in zip(grad_values, chains):
            grad_packed[rows, 2 * D + at : 2 * D + at + LANES] = grad.astype(jnp.bfloat16)
        inners = [
            jnp.sum(attend * grad, axis=0, keepdims=True)
            for attend, grad in zip(attends, grad_attends)
        ]
        grad_scores = [
            (attend * (grad - inner)).astype(jnp.bfloat16)
            for attend, grad, inner in zip(attends, grad_attends, inners)
        ]
        grad_keys = [
            dot(grad, block_diagonal(packed[rows, at : at + LANES], first_half), 1, 0) * factor
            for grad, (rows, at, _) in zip(grad_scores, chains)
        ]
        for grad, (rows, at, _) in zip(grad_keys, chains):
            grad_packed[rows, D + at : D + at + LANES] = grad.astype(jnp.bfloat16)
        grad_queries = [
            dot(grad, packed[rows, D + at : D + at + LANES], 0, 0)
            for grad, (rows, at, _) in zip(grad_scores, chains)
        ]
        for grad, (rows, at, _) in zip(grad_queries, chains):
            grad_packed[rows, at : at + LANES] = (own_halves(grad, first_half) * factor).astype(
                jnp.bfloat16
            )


def layer_kernel(flows, shard, *refs):
    me, counts = refs[:2]
    pieces = refs[2 : 2 + 4 * FLOWS]
    tokens, cotangent, result, grad_input = refs[2 + 4 * FLOWS : 6 + 4 * FLOWS]
    outputs = refs[6 + 4 * FLOWS : 6 + 6 * FLOWS]
    (
        flat,
        w_qkv,
        w_out,
        w_up,
        w_down,
        vectors,
        acc_qkv,
        acc_out,
        acc_up,
        acc_down,
        acc_vectors,
        packed,
        chance,
        mixed,
        grad_mixed,
        grad_packed,
    ) = refs[6 + 6 * FLOWS :]
    step = pl.program_id(0)
    samples = tokens.shape[0] // PATCHES

    @pl.when(step == 0)
    def _():
        unpack(me[0], pieces, flows, shard, flat, w_qkv, w_out, w_up, w_down, vectors)
        for ref in (acc_qkv, acc_out, acc_up, acc_down, acc_vectors):
            ref[...] = jnp.zeros_like(ref)

    def count(sample):
        return counts[step * samples + sample]

    def add_vector(name, values, at=0):
        index = VECTORS.index(name)
        acc_vectors[index : index + 1, at : at + values.shape[1]] += jnp.sum(
            values, axis=0, keepdims=True
        )

    inputs = tokens[...].astype(jnp.float32)
    hat_one, scale_one = normalize(inputs)
    gain_one = vector(vectors, "gain_one")
    normed_one = (hat_one * gain_one + vector(vectors, "shift_one")).astype(jnp.bfloat16)
    packed[...] = dot(normed_one, w_qkv[...], 1, 0).astype(jnp.bfloat16)
    attention(count, packed, chance, mixed)
    hidden = inputs + dot(mixed[...], w_out[...], 1, 0) + vector(vectors, "bias_out")

    hat_two, scale_two = normalize(hidden)
    gain_two = vector(vectors, "gain_two")
    normed_two = (hat_two * gain_two + vector(vectors, "shift_two")).astype(jnp.bfloat16)
    slots = lax.broadcasted_iota(jnp.int32, (PATCHES, 1), 0)
    visible = jnp.concatenate(
        [jnp.where(slots < count(sample), 1.0, 0.0) for sample in range(samples)], axis=0
    )
    grad_out = cotangent[...].astype(jnp.float32) * visible
    grad_out_low = grad_out.astype(jnp.bfloat16)
    add_vector("bias_down", grad_out)
    total = hidden + vector(vectors, "bias_down")
    grad_normed_two = jnp.zeros_like(hidden)
    bias_up = vector(vectors, "bias_up")
    for at in range(0, FF, COLUMNS):
        columns = slice(at, at + COLUMNS)
        upward = dot(normed_two, w_up[:, columns], 1, 0) + bias_up[:, columns]
        below = 0.5 * (1.0 + lax.erf(upward * 0.5**0.5))
        active = (upward * below).astype(jnp.bfloat16)
        slope = below + upward * (jnp.exp(-0.5 * upward * upward) * (0.5 / jnp.pi) ** 0.5)
        total = total + dot(active, w_down[columns, :], 1, 0)
        grad_upward = dot(grad_out_low, w_down[columns, :], 1, 1) * slope
        grad_upward = grad_upward.astype(jnp.bfloat16)
        add_vector("bias_up", grad_upward.astype(jnp.float32), at)
        acc_down[columns, :] += dot(active, grad_out_low, 0, 0)
        acc_up[:, columns] += dot(normed_two, grad_upward, 0, 0)
        grad_normed_two = grad_normed_two + dot(grad_upward, w_up[:, columns], 1, 1)
    result[...] = total.astype(jnp.bfloat16)
    add_vector("gain_two", grad_normed_two * hat_two)
    add_vector("shift_two", grad_normed_two)
    grad_hidden = grad_out + norm_back(grad_normed_two, gain_two, hat_two, scale_two)

    grad_hidden_low = grad_hidden.astype(jnp.bfloat16)
    add_vector("bias_out", grad_hidden_low.astype(jnp.float32))
    acc_out[...] += dot(mixed[...], grad_hidden_low, 0, 0)
    grad_mixed[...] = dot(grad_hidden_low, w_out[...], 1, 1).astype(jnp.bfloat16)
    attention_back(packed, chance, grad_mixed, grad_packed)
    acc_qkv[...] += dot(normed_one, grad_packed[...], 0, 0)
    grad_normed_one = dot(grad_packed[...], w_qkv[...], 1, 1)
    add_vector("gain_one", grad_normed_one * hat_one)
    add_vector("shift_one", grad_normed_one)
    grad_input[...] = (
        grad_hidden + norm_back(grad_normed_one, gain_one, hat_one, scale_one)
    ).astype(jnp.bfloat16)

    @pl.when(step == pl.num_programs(0) - 1)
    def _():
        pack(
            me[0], flows, shard, flat, acc_qkv, acc_out, acc_up, acc_down, acc_vectors, outputs
        )


def layer(me, counts, pieces, tokens, cotangent, flows, shard):
    rows = tokens.shape[0]
    block = min(BLOCK, rows)
    quarter, piece_rows, _ = pieces[0].shape
    devices = 4 * quarter
    flat_rows = first_row(devices - 1, shard) + FLOWS * piece_rows
    low = jnp.bfloat16
    full = jnp.float32

    def by_rows():
        return pl.BlockSpec((block, D), lambda i, me, counts: (i, 0))

    chunk_shape = (devices // 2, piece_rows, LANES)
    return pl.pallas_call(
        functools.partial(layer_kernel, flows, shard),
        name="layer",
        grid_spec=pltpu.PrefetchScalarGridSpec(
            num_scalar_prefetch=2,
            grid=(rows // block,),
            in_specs=[pl.BlockSpec(memory_space=pltpu.VMEM)] * len(pieces)
            + [by_rows(), by_rows()],
            out_specs=[by_rows(), by_rows()]
            + [pl.BlockSpec(memory_space=pltpu.VMEM)] * (2 * FLOWS),
            scratch_shapes=[
                pltpu.VMEM((flat_rows, LANES), full),
                pltpu.VMEM((D, 3 * D), low),
                pltpu.VMEM((D, D), low),
                pltpu.VMEM((D, FF), low),
                pltpu.VMEM((FF, D), low),
                pltpu.VMEM((8, FF), full),
                pltpu.VMEM((D, 3 * D), full),
                pltpu.VMEM((D, D), full),
                pltpu.VMEM((D, FF), full),
                pltpu.VMEM((FF, D), full),
                pltpu.VMEM((8, FF), full),
                pltpu.VMEM((block, 3 * D), low),
                pltpu.VMEM((block, D), full),
                pltpu.VMEM((block, D), low),
                pltpu.VMEM((block, D), low),
                pltpu.VMEM((block, 3 * D), low),
            ],
        ),
        out_shape=[jax.ShapeDtypeStruct((rows, D), low)] * 2
        + [pltpu.VMEM(chunk_shape, dtype) for dtype in (full, low)] * FLOWS,
        compiler_params=pltpu.CompilerParams(vmem_limit_bytes=VMEM_LIMIT),
    )(me, counts, *pieces, tokens, cotangent)


def step_scale(position):
    bound_one = QKV_ROWS * LANES
    bound_two = BASE_UP * LANES
    bound_three = BASE_DOWN * LANES
    bound_four = BASE_VEC * LANES
    scale = jnp.where(
        position < bound_one,
        D ** (-0.5),
        jnp.where(
            position < bound_two,
            (D // 8) ** (-0.5),
            jnp.where(
                position < bound_three,
                D ** (-0.5),
                jnp.where(position < bound_four, FF ** (-0.5), 0.1),
            ),
        ),
    )
    decay = jnp.where(position < bound_four, 0.05, 0.0)
    return (scale, decay)


def on_device(tokens, counts, cotangent, master, first, second, rate, step):
    shard = master.shape[0]
    me = lax.axis_index(AXES)
    sizes = (lax.axis_size("wide"), lax.axis_size("narrow"))
    flows = exchange_flows(*sizes)
    rows = chunk_rows(shard)
    offset = me * shard % 1024
    own = lax.dynamic_update_slice(
        jnp.zeros((rows * LANES,), jnp.bfloat16), master.astype(jnp.bfloat16), (offset,)
    ).reshape(FLOWS, rows // FLOWS, LANES)
    pieces = gather_chunks(own, flows)
    result, grad_input, *chunks = layer(
        me.reshape(1), counts, pieces, tokens, cotangent, flows, shard
    )
    reduced = jnp.concatenate(scatter_chunks(chunks, flows), axis=0)
    reduced = lax.dynamic_slice(reduced.reshape(rows * LANES), (offset,), (shard,))
    position = me * shard + jnp.arange(shard, dtype=jnp.int32)
    first_new = 0.5 * first + 0.5 * reduced
    second_new = 0.5 * second + 0.5 * reduced * reduced
    correct = 1.0 - jnp.power(jnp.float32(0.5), step[0].astype(jnp.float32))
    scale, decay = step_scale(position)
    moved = first_new / correct / (jnp.sqrt(second_new / correct) + 1e-08)
    master_new = master - rate[0] * scale * (moved + decay * master)
    return (
        result,
        grad_input,
        master_new,
        first_new,
        second_new,
        master_new.astype(jnp.bfloat16),
    )


def solution(mesh):
    split = P(AXES)
    by_rows = P(AXES, None)
    return jax.shard_map(
        on_device,
        mesh=mesh,
        in_specs=(by_rows, split, by_rows, split, split, split, P(), P()),
        out_specs=(by_rows, by_rows, split, split, split, split),
        check_vma=False,
    )
```

```python
import functools

import jax
import jax.numpy as jnp
from jax import lax
from jax.experimental import pallas as pl
from jax.experimental.pallas import tpu as pltpu
from jax.sharding import PartitionSpec as P

D = 384
FF = 1536
HEADS = 6
HEAD_DIM = 64
PATCHES = 64
LANES = 128
PAIRS = HEADS // 2
EPS = 1e-06
AXES = ("wide", "narrow")
QKV_ROWS = 3 * D * D // LANES
OUT_ROWS = D * D // LANES
UP_ROWS = D * FF // LANES
VEC_ROWS = (6 * D + FF) // LANES
FLAT_ROWS = QKV_ROWS + OUT_ROWS + 2 * UP_ROWS + VEC_ROWS
BASE_OUT = QKV_ROWS
BASE_UP = BASE_OUT + OUT_ROWS
BASE_DOWN = BASE_UP + UP_ROWS
BASE_VEC = BASE_DOWN + UP_ROWS
VECTORS = ("gain_one", "shift_one", "bias_out", "gain_two", "shift_two", "bias_up", "bias_down")
VMEM_LIMIT = 44 * 1024 * 1024
BLOCK = 512
GROUP = 8
COLUMNS = 512
FLOWS = 2


def round_up(value, step):
    return (value + step - 1) // step * step


def dot(left, right, left_dim, right_dim):
    return lax.dot_general(
        left, right, (((left_dim,), (right_dim,)), ((), ())), preferred_element_type=jnp.float32
    )


def chunk_rows(shard):
    return round_up(shard + 1024, 16 * FLOWS * LANES) // LANES


class Flow:
    def __init__(self, rounds, devices, core):
        self.swaps = [
            [(device, device ^ pair[1 if device & core else 0]) for device in range(devices)]
            for pair in rounds
        ]
        self.core_swap = [(device, device ^ core) for device in range(devices)]
        self.core = core
        half = devices // 2
        self.across = [[0] * devices, [0] * devices]
        for side in (0, 1):
            for slot in range(half):
                for index, pair in enumerate(rounds):
                    if slot >> index & 1:
                        self.across[side][slot] ^= pair[side]
                        self.across[1 - side][half + slot] ^= pair[side]
                self.across[1 - side][half + slot] ^= core

    def owner(self, me, slot):
        side_one = (me & self.core) != 0
        return me ^ jnp.where(side_one, self.across[1][slot], self.across[0][slot])


def exchange_flows(wide, narrow):
    bits = chip_bits(wide * narrow, narrow)
    top, middle, (first, second) = bits[:1], bits[1:-2], bits[-2:]
    orders = [
        (top + [second, first] + middle, [first] + top + middle + [second]),
        (top + middle + [first, second], [second] + middle + top + [first]),
    ]
    return [Flow(list(zip(*order)), wide * narrow, narrow) for order in orders]


def chip_bits(devices, core):
    return [1 << k for k in reversed(range(devices.bit_length() - 1)) if 1 << k != core]


def after(value, other):
    if other is None:
        return value
    return lax.optimization_barrier((value, other))[0]


def gather_chunks(owns, flows):
    held = [own[None] for own in owns]
    taken = [None] * len(flows)
    turns = list(reversed(range(len(flows))))
    last = None
    for index in range(len(flows[0].swaps)):
        for turn in turns:
            if index:
                held[turn] = jnp.concatenate([after(held[turn], last), taken[turn]], axis=0)
            last = held[turn]
            taken[turn] = lax.ppermute(last, AXES, flows[turn].swaps[index])
    pieces = []
    for flow, kept, new in zip(flows, held, taken):
        pieces += [kept, new]
        pieces += [lax.ppermute(piece, AXES, flow.core_swap) for piece in (kept, new)]
    return pieces


def scatter_chunks(chunks, flows):
    parts = [
        [kept, lax.ppermute(sent, AXES, flow.core_swap)]
        for kept, sent, flow in zip(chunks[::2], chunks[1::2], flows)
    ]
    last = None
    for index in reversed(range(len(flows[0].swaps))):
        for turn, flow in enumerate(flows):
            half = parts[turn][0].shape[0] // 2
            parts[turn][0] = after(parts[turn][0], last)
            upper = sum(part[half:].astype(jnp.float32) for part in parts[turn])
            last = upper.astype(jnp.bfloat16)
            parts[turn] = [part[:half] for part in parts[turn]]
            parts[turn].append(lax.ppermute(last, AXES, flow.swaps[index]))
    return [sum(part[0].astype(jnp.float32) for part in flow) for flow in parts]


def vector_width(name):
    return FF if name == "bias_up" else D


def vector_rows():
    row = BASE_VEC
    for index, name in enumerate(VECTORS):
        for block in range(vector_width(name) // LANES):
            yield index, slice(block * LANES, (block + 1) * LANES), row
            row += 1


def matrix_blocks(matrix, base):
    height, width = matrix.shape
    blocks = width // LANES
    for block in range(blocks):
        columns = slice(block * LANES, (block + 1) * LANES)
        yield columns, pl.ds(base + block, height, stride=blocks)


def first_row(owner, shard):
    return owner * shard // 1024 * 8


def dynamic_first_row(owner, shard):
    return pl.multiple_of(lax.shift_right_logical(owner * shard, 10) * 8, 8)


def unpack(me, pieces, flows, shard, flat, w_qkv, w_out, w_up, w_down, vectors):
    rows = pieces[0].shape[1]
    devices = 4 * pieces[0].shape[0]
    sure = shard // 1024 * 8
    for owner in range(devices):
        start = first_row(owner, shard)
        flat[start : start + 8, :] = jnp.zeros((8, LANES), jnp.float32)
        flat[start + sure : start + FLOWS * rows, :] = jnp.zeros(
            (FLOWS * rows - sure, LANES), jnp.float32
        )
    for index, flow in enumerate(flows):
        low, high = index * rows, (index + 1) * rows
        cuts = sorted({low, high} | {cut for cut in (8, sure) if low < cut < high})
        for slot in range(devices):
            source = pieces[4 * index + slot * 4 // devices]
            start = dynamic_first_row(flow.owner(me, slot), shard)
            for begin, end in zip(cuts, cuts[1:]):
                piece = source[slot % source.shape[0], begin - low : end - low, :]
                piece = piece.astype(jnp.float32)
                target = (pl.ds(pl.multiple_of(start + begin, 8), end - begin), slice(None))
                if begin < 8 or begin >= sure:
                    flat[target] += piece
                else:
                    flat[target] = piece
    for matrix, base in ((w_qkv, 0), (w_out, BASE_OUT), (w_up, BASE_UP), (w_down, BASE_DOWN)):
        for columns, rows_of in matrix_blocks(matrix, base):
            matrix[:, columns] = flat[rows_of, :].astype(jnp.bfloat16)
    for index, columns, row in vector_rows():
        vectors[index : index + 1, columns] = flat[row : row + 1, :]


def pack(me, flows, shard, flat, grad_qkv, grad_out, grad_up, grad_down, vectors, outputs):
    for matrix, base in (
        (grad_qkv, 0),
        (grad_out, BASE_OUT),
        (grad_up, BASE_UP),
        (grad_down, BASE_DOWN),
    ):
        for columns, rows_of in matrix_blocks(matrix, base):
            flat[rows_of, :] = matrix[:, columns]
    for index, columns, row in vector_rows():
        flat[row : row + 1, :] = vectors[index : index + 1, columns]
    flat[FLAT_ROWS:, :] = jnp.zeros((flat.shape[0] - FLAT_ROWS, LANES), jnp.float32)
    for index, flow in enumerate(flows):
        kept, sent = outputs[2 * index : 2 * index + 2]
        half, rows, _ = kept.shape
        for slot in range(half):
            start = dynamic_first_row(flow.owner(me, slot), shard) + index * rows
            kept[slot] = flat[pl.ds(pl.multiple_of(start, 8), rows), :]
            start = dynamic_first_row(flow.owner(me, half + slot), shard) + index * rows
            sent[slot] = flat[pl.ds(pl.multiple_of(start, 8), rows), :].astype(jnp.bfloat16)


def vector(vectors, name):
    index = VECTORS.index(name)
    return vectors[index : index + 1, : vector_width(name)]


def normalize(values):
    center = values - jnp.mean(values, axis=-1, keepdims=True)
    spread = jnp.mean(center * center, axis=-1, keepdims=True)
    scale = lax.rsqrt(spread + EPS)
    return center * scale, scale


def norm_back(grad, gain, hat, scale):
    inner = grad * gain
    mean_inner = jnp.mean(inner, axis=-1, keepdims=True)
    mean_cross = jnp.mean(inner * hat, axis=-1, keepdims=True)
    return scale * (inner - mean_inner - hat * mean_cross)


def first_halves():
    return lax.broadcasted_iota(jnp.int32, (PATCHES, LANES), 1) < HEAD_DIM


def block_diagonal(values, first_half):
    zero = jnp.zeros_like(values)
    return jnp.concatenate(
        [jnp.where(first_half, values, zero), jnp.where(first_half, zero, values)], axis=0
    )


def own_halves(values, first_half):
    return jnp.where(first_half, values[:PATCHES], values[PATCHES:])


def head_chains(samples):
    for sample in range(0, samples, GROUP):
        yield [
            (slice(each * PATCHES, (each + 1) * PATCHES), pair * LANES, each)
            for each in range(sample, min(sample + GROUP, samples))
            for pair in range(PAIRS)
        ]


def attention(count, packed, chance, mixed):
    first_half = first_halves()
    slots = lax.broadcasted_iota(jnp.int32, (PATCHES, LANES), 0)
    for chains in head_chains(packed.shape[0] // PATCHES):
        scores = [
            dot(
                packed[rows, D + at : D + at + LANES],
                block_diagonal(packed[rows, at : at + LANES], first_half),
                1,
                1,
            )
            for rows, at, _ in chains
        ]
        scores = [
            jnp.where(slots < count(each), score * HEAD_DIM**-0.5, -1e30)
            for score, (_, _, each) in zip(scores, chains)
        ]
        exponents = [jnp.exp(score - jnp.max(score, axis=0, keepdims=True)) for score in scores]
        attends = [
            exponent * (1.0 / jnp.sum(exponent, axis=0, keepdims=True)) for exponent in exponents
        ]
        for attend, (rows, at, _) in zip(attends, chains):
            chance[rows, at : at + LANES] = attend
        mixes = [
            dot(attend.astype(jnp.bfloat16), packed[rows, 2 * D + at : 2 * D + at + LANES], 0, 0)
            for attend, (rows, at, _) in zip(attends, chains)
        ]
        for mix, (rows, at, _) in zip(mixes, chains):
            mixed[rows, at : at + LANES] = own_halves(mix, first_half).astype(jnp.bfloat16)


def attention_back(packed, chance, grad_mixed, grad_packed):
    first_half = first_halves()
    factor = HEAD_DIM**-0.5
    for chains in head_chains(packed.shape[0] // PATCHES):
        sides = [
            block_diagonal(grad_mixed[rows, at : at + LANES], first_half) for rows, at, _ in chains
        ]
        grad_attends = [
            dot(packed[rows, 2 * D + at : 2 * D + at + LANES], side, 1, 1)
            for side, (rows, at, _) in zip(sides, chains)
        ]
        attends = [chance[rows, at : at + LANES] for rows, at, _ in chains]
        grad_values = [
            dot(attend.astype(jnp.bfloat16), side, 1, 0) for attend, side in zip(attends, sides)
        ]
        for grad, (rows, at, _) in zip(grad_values, chains):
            grad_packed[rows, 2 * D + at : 2 * D + at + LANES] = grad.astype(jnp.bfloat16)
        inners = [
            jnp.sum(attend * grad, axis=0, keepdims=True)
            for attend, grad in zip(attends, grad_attends)
        ]
        grad_scores = [
            (attend * (grad - inner)).astype(jnp.bfloat16)
            for attend, grad, inner in zip(attends, grad_attends, inners)
        ]
        grad_keys = [
            dot(grad, block_diagonal(packed[rows, at : at + LANES], first_half), 1, 0) * factor
            for grad, (rows, at, _) in zip(grad_scores, chains)
        ]
        for grad, (rows, at, _) in zip(grad_keys, chains):
            grad_packed[rows, D + at : D + at + LANES] = grad.astype(jnp.bfloat16)
        grad_queries = [
            dot(grad, packed[rows, D + at : D + at + LANES], 0, 0)
            for grad, (rows, at, _) in zip(grad_scores, chains)
        ]
        for grad, (rows, at, _) in zip(grad_queries, chains):
            grad_packed[rows, at : at + LANES] = (own_halves(grad, first_half) * factor).astype(
                jnp.bfloat16
            )


def layer_kernel(flows, shard, *refs):
    me, counts = refs[:2]
    pieces = refs[2 : 2 + 4 * FLOWS]
    tokens, cotangent, result, grad_input = refs[2 + 4 * FLOWS : 6 + 4 * FLOWS]
    outputs = refs[6 + 4 * FLOWS : 6 + 6 * FLOWS]
    (
        flat,
        w_qkv,
        w_out,
        w_up,
        w_down,
        vectors,
        acc_qkv,
        acc_out,
        acc_up,
        acc_down,
        acc_vectors,
        packed,
        chance,
        mixed,
        grad_mixed,
        grad_packed,
    ) = refs[6 + 6 * FLOWS :]
    step = pl.program_id(0)
    samples = tokens.shape[0] // PATCHES

    @pl.when(step == 0)
    def _():
        unpack(me[0], pieces, flows, shard, flat, w_qkv, w_out, w_up, w_down, vectors)
        for ref in (acc_qkv, acc_out, acc_up, acc_down, acc_vectors):
            ref[...] = jnp.zeros_like(ref)

    def count(sample):
        return counts[step * samples + sample]

    def add_vector(name, values, at=0):
        index = VECTORS.index(name)
        acc_vectors[index : index + 1, at : at + values.shape[1]] += jnp.sum(
            values, axis=0, keepdims=True
        )

    inputs = tokens[...].astype(jnp.float32)
    hat_one, scale_one = normalize(inputs)
    gain_one = vector(vectors, "gain_one")
    normed_one = (hat_one * gain_one + vector(vectors, "shift_one")).astype(jnp.bfloat16)
    packed[...] = dot(normed_one, w_qkv[...], 1, 0).astype(jnp.bfloat16)
    attention(count, packed, chance, mixed)
    hidden = inputs + dot(mixed[...], w_out[...], 1, 0) + vector(vectors, "bias_out")

    hat_two, scale_two = normalize(hidden)
    gain_two = vector(vectors, "gain_two")
    normed_two = (hat_two * gain_two + vector(vectors, "shift_two")).astype(jnp.bfloat16)
    slots = lax.broadcasted_iota(jnp.int32, (PATCHES, 1), 0)
    visible = jnp.concatenate(
        [jnp.where(slots < count(sample), 1.0, 0.0) for sample in range(samples)], axis=0
    )
    grad_out = cotangent[...].astype(jnp.float32) * visible
    grad_out_low = grad_out.astype(jnp.bfloat16)
    add_vector("bias_down", grad_out)
    total = hidden + vector(vectors, "bias_down")
    grad_normed_two = jnp.zeros_like(hidden)
    bias_up = vector(vectors, "bias_up")
    for at in range(0, FF, COLUMNS):
        columns = slice(at, at + COLUMNS)
        upward = dot(normed_two, w_up[:, columns], 1, 0) + bias_up[:, columns]
        below = 0.5 * (1.0 + lax.erf(upward * 0.5**0.5))
        active = (upward * below).astype(jnp.bfloat16)
        slope = below + upward * (jnp.exp(-0.5 * upward * upward) * (0.5 / jnp.pi) ** 0.5)
        total = total + dot(active, w_down[columns, :], 1, 0)
        grad_upward = dot(grad_out_low, w_down[columns, :], 1, 1) * slope
        grad_upward = grad_upward.astype(jnp.bfloat16)
        add_vector("bias_up", grad_upward.astype(jnp.float32), at)
        acc_down[columns, :] += dot(active, grad_out_low, 0, 0)
        acc_up[:, columns] += dot(normed_two, grad_upward, 0, 0)
        grad_normed_two = grad_normed_two + dot(grad_upward, w_up[:, columns], 1, 1)
    result[...] = total.astype(jnp.bfloat16)
    add_vector("gain_two", grad_normed_two * hat_two)
    add_vector("shift_two", grad_normed_two)
    grad_hidden = grad_out + norm_back(grad_normed_two, gain_two, hat_two, scale_two)

    grad_hidden_low = grad_hidden.astype(jnp.bfloat16)
    add_vector("bias_out", grad_hidden_low.astype(jnp.float32))
    acc_out[...] += dot(mixed[...], grad_hidden_low, 0, 0)
    grad_mixed[...] = dot(grad_hidden_low, w_out[...], 1, 1).astype(jnp.bfloat16)
    attention_back(packed, chance, grad_mixed, grad_packed)
    acc_qkv[...] += dot(normed_one, grad_packed[...], 0, 0)
    grad_normed_one = dot(grad_packed[...], w_qkv[...], 1, 1)
    add_vector("gain_one", grad_normed_one * hat_one)
    add_vector("shift_one", grad_normed_one)
    grad_input[...] = (
        grad_hidden + norm_back(grad_normed_one, gain_one, hat_one, scale_one)
    ).astype(jnp.bfloat16)

    @pl.when(step == pl.num_programs(0) - 1)
    def _():
        pack(
            me[0], flows, shard, flat, acc_qkv, acc_out, acc_up, acc_down, acc_vectors, outputs
        )


def layer(me, counts, pieces, tokens, cotangent, flows, shard):
    rows = tokens.shape[0]
    block = min(BLOCK, rows)
    quarter, piece_rows, _ = pieces[0].shape
    devices = 4 * quarter
    flat_rows = first_row(devices - 1, shard) + FLOWS * piece_rows
    low = jnp.bfloat16
    full = jnp.float32

    def by_rows():
        return pl.BlockSpec((block, D), lambda i, me, counts: (i, 0))

    chunk_shape = (devices // 2, piece_rows, LANES)
    return pl.pallas_call(
        functools.partial(layer_kernel, flows, shard),
        name="layer",
        grid_spec=pltpu.PrefetchScalarGridSpec(
            num_scalar_prefetch=2,
            grid=(rows // block,),
            in_specs=[pl.BlockSpec(memory_space=pltpu.VMEM)] * len(pieces)
            + [by_rows(), by_rows()],
            out_specs=[by_rows(), by_rows()]
            + [pl.BlockSpec(memory_space=pltpu.VMEM)] * (2 * FLOWS),
            scratch_shapes=[
                pltpu.VMEM((flat_rows, LANES), full),
                pltpu.VMEM((D, 3 * D), low),
                pltpu.VMEM((D, D), low),
                pltpu.VMEM((D, FF), low),
                pltpu.VMEM((FF, D), low),
                pltpu.VMEM((8, FF), full),
                pltpu.VMEM((D, 3 * D), full),
                pltpu.VMEM((D, D), full),
                pltpu.VMEM((D, FF), full),
                pltpu.VMEM((FF, D), full),
                pltpu.VMEM((8, FF), full),
                pltpu.VMEM((block, 3 * D), low),
                pltpu.VMEM((block, D), full),
                pltpu.VMEM((block, D), low),
                pltpu.VMEM((block, D), low),
                pltpu.VMEM((block, 3 * D), low),
            ],
        ),
        out_shape=[jax.ShapeDtypeStruct((rows, D), low)] * 2
        + [pltpu.VMEM(chunk_shape, dtype) for dtype in (full, low)] * FLOWS,
        compiler_params=pltpu.CompilerParams(vmem_limit_bytes=VMEM_LIMIT),
    )(me, counts, *pieces, tokens, cotangent)


def step_scale(position):
    bound_one = QKV_ROWS * LANES
    bound_two = BASE_UP * LANES
    bound_three = BASE_DOWN * LANES
    bound_four = BASE_VEC * LANES
    scale = jnp.where(
        position < bound_one,
        D ** (-0.5),
        jnp.where(
            position < bound_two,
            (D // 8) ** (-0.5),
            jnp.where(
                position < bound_three,
                D ** (-0.5),
                jnp.where(position < bound_four, FF ** (-0.5), 0.1),
            ),
        ),
    )
    decay = jnp.where(position < bound_four, 0.05, 0.0)
    return (scale, decay)


def on_device(tokens, counts, cotangent, master, first, second, rate, step):
    shard = master.shape[0]
    me = lax.axis_index(AXES)
    sizes = (lax.axis_size("wide"), lax.axis_size("narrow"))
    flows = exchange_flows(*sizes)
    rows = chunk_rows(shard)
    offset = me * shard % 1024
    own = lax.dynamic_update_slice(
        jnp.zeros((rows * LANES,), jnp.bfloat16), master.astype(jnp.bfloat16), (offset,)
    ).reshape(FLOWS, rows // FLOWS, LANES)
    pieces = gather_chunks(own, flows)
    result, grad_input, *chunks = layer(
        me.reshape(1), counts, pieces, tokens, cotangent, flows, shard
    )
    reduced = jnp.concatenate(scatter_chunks(chunks, flows), axis=0)
    reduced = lax.dynamic_slice(reduced.reshape(rows * LANES), (offset,), (shard,))
    position = me * shard + jnp.arange(shard, dtype=jnp.int32)
    first_new = 0.5 * first + 0.5 * reduced
    second_new = 0.5 * second + 0.5 * reduced * reduced
    correct = 1.0 - jnp.power(jnp.float32(0.5), step[0].astype(jnp.float32))
    scale, decay = step_scale(position)
    moved = first_new / correct / (jnp.sqrt(second_new / correct) + 1e-08)
    master_new = master - rate[0] * scale * (moved + decay * master)
    return (
        result,
        grad_input,
        master_new,
        first_new,
        second_new,
        master_new.astype(jnp.bfloat16),
    )


def solution(mesh):
    split = P(AXES)
    by_rows = P(AXES, None)
    return jax.shard_map(
        on_device,
        mesh=mesh,
        in_specs=(by_rows, split, by_rows, split, split, split, P(), P()),
        out_specs=(by_rows, by_rows, split, split, split, split),
        check_vma=False,
    )
```

```python
import functools

import jax
import jax.numpy as jnp
from jax import lax
from jax.experimental import pallas as pl
from jax.experimental.pallas import tpu as pltpu
from jax.sharding import PartitionSpec as P

D = 384
FF = 1536
HEADS = 6
HEAD_DIM = 64
PATCHES = 64
LANES = 128
PAIRS = HEADS // 2
EPS = 1e-06
AXES = ("wide", "narrow")
QKV_ROWS = 3 * D * D // LANES
OUT_ROWS = D * D // LANES
UP_ROWS = D * FF // LANES
VEC_ROWS = (6 * D + FF) // LANES
FLAT_ROWS = QKV_ROWS + OUT_ROWS + 2 * UP_ROWS + VEC_ROWS
BASE_OUT = QKV_ROWS
BASE_UP = BASE_OUT + OUT_ROWS
BASE_DOWN = BASE_UP + UP_ROWS
BASE_VEC = BASE_DOWN + UP_ROWS
VECTORS = ("gain_one", "shift_one", "bias_out", "gain_two", "shift_two", "bias_up", "bias_down")
VMEM_LIMIT = 44 * 1024 * 1024
BLOCK = 512
GROUP = 8
COLUMNS = 768
FLOWS = 2


def round_up(value, step):
    return (value + step - 1) // step * step


def dot(left, right, left_dim, right_dim):
    return lax.dot_general(
        left, right, (((left_dim,), (right_dim,)), ((), ())), preferred_element_type=jnp.float32
    )


def chunk_rows(shard):
    return round_up(shard + 1024, 16 * FLOWS * LANES) // LANES


class Flow:
    def __init__(self, rounds, devices, core):
        self.swaps = [
            [(device, device ^ pair[1 if device & core else 0]) for device in range(devices)]
            for pair in rounds
        ]
        self.core_swap = [(device, device ^ core) for device in range(devices)]
        self.core = core
        half = devices // 2
        self.across = [[0] * devices, [0] * devices]
        for side in (0, 1):
            for slot in range(half):
                for index, pair in enumerate(rounds):
                    if slot >> index & 1:
                        self.across[side][slot] ^= pair[side]
                        self.across[1 - side][half + slot] ^= pair[side]
                self.across[1 - side][half + slot] ^= core

    def owner(self, me, slot):
        side_one = (me & self.core) != 0
        return me ^ jnp.where(side_one, self.across[1][slot], self.across[0][slot])


def exchange_flows(wide, narrow):
    bits = chip_bits(wide * narrow, narrow)
    top, middle, (first, second) = bits[:1], bits[1:-2], bits[-2:]
    orders = [
        (top + [second, first] + middle, [first] + top + middle + [second]),
        (top + middle + [first, second], [second] + middle + top + [first]),
    ]
    return [Flow(list(zip(*order)), wide * narrow, narrow) for order in orders]


def chip_bits(devices, core):
    return [1 << k for k in reversed(range(devices.bit_length() - 1)) if 1 << k != core]


def after(value, other):
    if other is None:
        return value
    return lax.optimization_barrier((value, other))[0]


def gather_chunks(owns, flows):
    held = [own[None] for own in owns]
    taken = [None] * len(flows)
    turns = list(reversed(range(len(flows))))
    last = None
    for index in range(len(flows[0].swaps)):
        for turn in turns:
            if index:
                held[turn] = jnp.concatenate([after(held[turn], last), taken[turn]], axis=0)
            last = held[turn]
            taken[turn] = lax.ppermute(last, AXES, flows[turn].swaps[index])
    pieces = []
    for flow, kept, new in zip(flows, held, taken):
        pieces += [kept, new]
        pieces += [lax.ppermute(piece, AXES, flow.core_swap) for piece in (kept, new)]
    return pieces


def scatter_chunks(chunks, flows):
    parts = [
        [kept, lax.ppermute(sent, AXES, flow.core_swap)]
        for kept, sent, flow in zip(chunks[::2], chunks[1::2], flows)
    ]
    last = None
    for index in reversed(range(len(flows[0].swaps))):
        for turn, flow in enumerate(flows):
            half = parts[turn][0].shape[0] // 2
            parts[turn][0] = after(parts[turn][0], last)
            upper = sum(part[half:].astype(jnp.float32) for part in parts[turn])
            last = upper.astype(jnp.bfloat16)
            parts[turn] = [part[:half] for part in parts[turn]]
            parts[turn].append(lax.ppermute(last, AXES, flow.swaps[index]))
    return [sum(part[0].astype(jnp.float32) for part in flow) for flow in parts]


def vector_width(name):
    return FF if name == "bias_up" else D


def vector_rows():
    row = BASE_VEC
    for index, name in enumerate(VECTORS):
        for block in range(vector_width(name) // LANES):
            yield index, slice(block * LANES, (block + 1) * LANES), row
            row += 1


def matrix_blocks(matrix, base):
    height, width = matrix.shape
    blocks = width // LANES
    for block in range(blocks):
        columns = slice(block * LANES, (block + 1) * LANES)
        yield columns, pl.ds(base + block, height, stride=blocks)


def first_row(owner, shard):
    return owner * shard // 1024 * 8


def dynamic_first_row(owner, shard):
    return pl.multiple_of(lax.shift_right_logical(owner * shard, 10) * 8, 8)


def unpack(me, pieces, flows, shard, flat, w_qkv, w_out, w_up, w_down, vectors):
    rows = pieces[0].shape[1]
    devices = 4 * pieces[0].shape[0]
    sure = shard // 1024 * 8
    for owner in range(devices):
        start = first_row(owner, shard)
        flat[start : start + 8, :] = jnp.zeros((8, LANES), jnp.float32)
        flat[start + sure : start + FLOWS * rows, :] = jnp.zeros(
            (FLOWS * rows - sure, LANES), jnp.float32
        )
    for index, flow in enumerate(flows):
        low, high = index * rows, (index + 1) * rows
        cuts = sorted({low, high} | {cut for cut in (8, sure) if low < cut < high})
        for slot in range(devices):
            source = pieces[4 * index + slot * 4 // devices]
            start = dynamic_first_row(flow.owner(me, slot), shard)
            for begin, end in zip(cuts, cuts[1:]):
                piece = source[slot % source.shape[0], begin - low : end - low, :]
                piece = piece.astype(jnp.float32)
                target = (pl.ds(pl.multiple_of(start + begin, 8), end - begin), slice(None))
                if begin < 8 or begin >= sure:
                    flat[target] += piece
                else:
                    flat[target] = piece
    for matrix, base in ((w_qkv, 0), (w_out, BASE_OUT), (w_up, BASE_UP), (w_down, BASE_DOWN)):
        for columns, rows_of in matrix_blocks(matrix, base):
            matrix[:, columns] = flat[rows_of, :].astype(jnp.bfloat16)
    for index, columns, row in vector_rows():
        vectors[index : index + 1, columns] = flat[row : row + 1, :]


def pack(me, flows, shard, flat, grad_qkv, grad_out, grad_up, grad_down, vectors, outputs):
    for matrix, base in (
        (grad_qkv, 0),
        (grad_out, BASE_OUT),
        (grad_up, BASE_UP),
        (grad_down, BASE_DOWN),
    ):
        for columns, rows_of in matrix_blocks(matrix, base):
            flat[rows_of, :] = matrix[:, columns]
    for index, columns, row in vector_rows():
        flat[row : row + 1, :] = vectors[index : index + 1, columns]
    flat[FLAT_ROWS:, :] = jnp.zeros((flat.shape[0] - FLAT_ROWS, LANES), jnp.float32)
    for index, flow in enumerate(flows):
        kept, sent = outputs[2 * index : 2 * index + 2]
        half, rows, _ = kept.shape
        for slot in range(half):
            start = dynamic_first_row(flow.owner(me, slot), shard) + index * rows
            kept[slot] = flat[pl.ds(pl.multiple_of(start, 8), rows), :]
            start = dynamic_first_row(flow.owner(me, half + slot), shard) + index * rows
            sent[slot] = flat[pl.ds(pl.multiple_of(start, 8), rows), :].astype(jnp.bfloat16)


def vector(vectors, name):
    index = VECTORS.index(name)
    return vectors[index : index + 1, : vector_width(name)]


def normalize(values):
    center = values - jnp.mean(values, axis=-1, keepdims=True)
    spread = jnp.mean(center * center, axis=-1, keepdims=True)
    scale = lax.rsqrt(spread + EPS)
    return center * scale, scale


def norm_back(grad, gain, hat, scale):
    inner = grad * gain
    mean_inner = jnp.mean(inner, axis=-1, keepdims=True)
    mean_cross = jnp.mean(inner * hat, axis=-1, keepdims=True)
    return scale * (inner - mean_inner - hat * mean_cross)


def first_halves():
    return lax.broadcasted_iota(jnp.int32, (PATCHES, LANES), 1) < HEAD_DIM


def block_diagonal(values, first_half):
    zero = jnp.zeros_like(values)
    return jnp.concatenate(
        [jnp.where(first_half, values, zero), jnp.where(first_half, zero, values)], axis=0
    )


def own_halves(values, first_half):
    return jnp.where(first_half, values[:PATCHES], values[PATCHES:])


def head_chains(samples):
    for sample in range(0, samples, GROUP):
        yield [
            (slice(each * PATCHES, (each + 1) * PATCHES), pair * LANES, each)
            for each in range(sample, min(sample + GROUP, samples))
            for pair in range(PAIRS)
        ]


def attention(count, packed, chance, mixed):
    first_half = first_halves()
    slots = lax.broadcasted_iota(jnp.int32, (PATCHES, LANES), 0)
    for chains in head_chains(packed.shape[0] // PATCHES):
        scores = [
            dot(
                packed[rows, D + at : D + at + LANES],
                block_diagonal(packed[rows, at : at + LANES], first_half),
                1,
                1,
            )
            for rows, at, _ in chains
        ]
        scores = [
            jnp.where(slots < count(each), score * HEAD_DIM**-0.5, -1e30)
            for score, (_, _, each) in zip(scores, chains)
        ]
        exponents = [jnp.exp(score - jnp.max(score, axis=0, keepdims=True)) for score in scores]
        attends = [
            exponent * (1.0 / jnp.sum(exponent, axis=0, keepdims=True)) for exponent in exponents
        ]
        for attend, (rows, at, _) in zip(attends, chains):
            chance[rows, at : at + LANES] = attend
        mixes = [
            dot(attend.astype(jnp.bfloat16), packed[rows, 2 * D + at : 2 * D + at + LANES], 0, 0)
            for attend, (rows, at, _) in zip(attends, chains)
        ]
        for mix, (rows, at, _) in zip(mixes, chains):
            mixed[rows, at : at + LANES] = own_halves(mix, first_half).astype(jnp.bfloat16)


def attention_back(packed, chance, grad_mixed, grad_packed):
    first_half = first_halves()
    factor = HEAD_DIM**-0.5
    for chains in head_chains(packed.shape[0] // PATCHES):
        sides = [
            block_diagonal(grad_mixed[rows, at : at + LANES], first_half) for rows, at, _ in chains
        ]
        grad_attends = [
            dot(packed[rows, 2 * D + at : 2 * D + at + LANES], side, 1, 1)
            for side, (rows, at, _) in zip(sides, chains)
        ]
        attends = [chance[rows, at : at + LANES] for rows, at, _ in chains]
        grad_values = [
            dot(attend.astype(jnp.bfloat16), side, 1, 0) for attend, side in zip(attends, sides)
        ]
        for grad, (rows, at, _) in zip(grad_values, chains):
            grad_packed[rows, 2 * D + at : 2 * D + at + LANES] = grad.astype(jnp.bfloat16)
        inners = [
            jnp.sum(attend * grad, axis=0, keepdims=True)
            for attend, grad in zip(attends, grad_attends)
        ]
        grad_scores = [
            (attend * (grad - inner)).astype(jnp.bfloat16)
            for attend, grad, inner in zip(attends, grad_attends, inners)
        ]
        grad_keys = [
            dot(grad, block_diagonal(packed[rows, at : at + LANES], first_half), 1, 0) * factor
            for grad, (rows, at, _) in zip(grad_scores, chains)
        ]
        for grad, (rows, at, _) in zip(grad_keys, chains):
            grad_packed[rows, D + at : D + at + LANES] = grad.astype(jnp.bfloat16)
        grad_queries = [
            dot(grad, packed[rows, D + at : D + at + LANES], 0, 0)
            for grad, (rows, at, _) in zip(grad_scores, chains)
        ]
        for grad, (rows, at, _) in zip(grad_queries, chains):
            grad_packed[rows, at : at + LANES] = (own_halves(grad, first_half) * factor).astype(
                jnp.bfloat16
            )


def layer_kernel(flows, shard, *refs):
    me, counts = refs[:2]
    pieces = refs[2 : 2 + 4 * FLOWS]
    tokens, cotangent, result, grad_input = refs[2 + 4 * FLOWS : 6 + 4 * FLOWS]
    outputs = refs[6 + 4 * FLOWS : 6 + 6 * FLOWS]
    (
        flat,
        w_qkv,
        w_out,
        w_up,
        w_down,
        vectors,
        acc_qkv,
        acc_out,
        acc_up,
        acc_down,
        acc_vectors,
        packed,
        chance,
        mixed,
        grad_mixed,
        grad_packed,
    ) = refs[6 + 6 * FLOWS :]
    step = pl.program_id(0)
    samples = tokens.shape[0] // PATCHES

    @pl.when(step == 0)
    def _():
        unpack(me[0], pieces, flows, shard, flat, w_qkv, w_out, w_up, w_down, vectors)
        for ref in (acc_qkv, acc_out, acc_up, acc_down, acc_vectors):
            ref[...] = jnp.zeros_like(ref)

    def count(sample):
        return counts[step * samples + sample]

    def add_vector(name, values, at=0):
        index = VECTORS.index(name)
        acc_vectors[index : index + 1, at : at + values.shape[1]] += jnp.sum(
            values, axis=0, keepdims=True
        )

    inputs = tokens[...].astype(jnp.float32)
    hat_one, scale_one = normalize(inputs)
    gain_one = vector(vectors, "gain_one")
    normed_one = (hat_one * gain_one + vector(vectors, "shift_one")).astype(jnp.bfloat16)
    packed[...] = dot(normed_one, w_qkv[...], 1, 0).astype(jnp.bfloat16)
    attention(count, packed, chance, mixed)
    hidden = inputs + dot(mixed[...], w_out[...], 1, 0) + vector(vectors, "bias_out")

    hat_two, scale_two = normalize(hidden)
    gain_two = vector(vectors, "gain_two")
    normed_two = (hat_two * gain_two + vector(vectors, "shift_two")).astype(jnp.bfloat16)
    slots = lax.broadcasted_iota(jnp.int32, (PATCHES, 1), 0)
    visible = jnp.concatenate(
        [jnp.where(slots < count(sample), 1.0, 0.0) for sample in range(samples)], axis=0
    )
    grad_out = cotangent[...].astype(jnp.float32) * visible
    grad_out_low = grad_out.astype(jnp.bfloat16)
    add_vector("bias_down", grad_out)
    total = hidden + vector(vectors, "bias_down")
    grad_normed_two = jnp.zeros_like(hidden)
    bias_up = vector(vectors, "bias_up")
    for at in range(0, FF, COLUMNS):
        columns = slice(at, at + COLUMNS)
        upward = dot(normed_two, w_up[:, columns], 1, 0) + bias_up[:, columns]
        below = 0.5 * (1.0 + lax.erf(upward * 0.5**0.5))
        active = (upward * below).astype(jnp.bfloat16)
        slope = below + upward * (jnp.exp(-0.5 * upward * upward) * (0.5 / jnp.pi) ** 0.5)
        total = total + dot(active, w_down[columns, :], 1, 0)
        grad_upward = dot(grad_out_low, w_down[columns, :], 1, 1) * slope
        grad_upward = grad_upward.astype(jnp.bfloat16)
        add_vector("bias_up", grad_upward.astype(jnp.float32), at)
        acc_down[columns, :] += dot(active, grad_out_low, 0, 0)
        acc_up[:, columns] += dot(normed_two, grad_upward, 0, 0)
        grad_normed_two = grad_normed_two + dot(grad_upward, w_up[:, columns], 1, 1)
    result[...] = total.astype(jnp.bfloat16)
    add_vector("gain_two", grad_normed_two * hat_two)
    add_vector("shift_two", grad_normed_two)
    grad_hidden = grad_out + norm_back(grad_normed_two, gain_two, hat_two, scale_two)

    grad_hidden_low = grad_hidden.astype(jnp.bfloat16)
    add_vector("bias_out", grad_hidden_low.astype(jnp.float32))
    acc_out[...] += dot(mixed[...], grad_hidden_low, 0, 0)
    grad_mixed[...] = dot(grad_hidden_low, w_out[...], 1, 1).astype(jnp.bfloat16)
    attention_back(packed, chance, grad_mixed, grad_packed)
    acc_qkv[...] += dot(normed_one, grad_packed[...], 0, 0)
    grad_normed_one = dot(grad_packed[...], w_qkv[...], 1, 1)
    add_vector("gain_one", grad_normed_one * hat_one)
    add_vector("shift_one", grad_normed_one)
    grad_input[...] = (
        grad_hidden + norm_back(grad_normed_one, gain_one, hat_one, scale_one)
    ).astype(jnp.bfloat16)

    @pl.when(step == pl.num_programs(0) - 1)
    def _():
        pack(
            me[0], flows, shard, flat, acc_qkv, acc_out, acc_up, acc_down, acc_vectors, outputs
        )


def layer(me, counts, pieces, tokens, cotangent, flows, shard):
    rows = tokens.shape[0]
    block = min(BLOCK, rows)
    quarter, piece_rows, _ = pieces[0].shape
    devices = 4 * quarter
    flat_rows = first_row(devices - 1, shard) + FLOWS * piece_rows
    low = jnp.bfloat16
    full = jnp.float32

    def by_rows():
        return pl.BlockSpec((block, D), lambda i, me, counts: (i, 0))

    chunk_shape = (devices // 2, piece_rows, LANES)
    return pl.pallas_call(
        functools.partial(layer_kernel, flows, shard),
        name="layer",
        grid_spec=pltpu.PrefetchScalarGridSpec(
            num_scalar_prefetch=2,
            grid=(rows // block,),
            in_specs=[pl.BlockSpec(memory_space=pltpu.VMEM)] * len(pieces)
            + [by_rows(), by_rows()],
            out_specs=[by_rows(), by_rows()]
            + [pl.BlockSpec(memory_space=pltpu.VMEM)] * (2 * FLOWS),
            scratch_shapes=[
                pltpu.VMEM((flat_rows, LANES), full),
                pltpu.VMEM((D, 3 * D), low),
                pltpu.VMEM((D, D), low),
                pltpu.VMEM((D, FF), low),
                pltpu.VMEM((FF, D), low),
                pltpu.VMEM((8, FF), full),
                pltpu.VMEM((D, 3 * D), full),
                pltpu.VMEM((D, D), full),
                pltpu.VMEM((D, FF), full),
                pltpu.VMEM((FF, D), full),
                pltpu.VMEM((8, FF), full),
                pltpu.VMEM((block, 3 * D), low),
                pltpu.VMEM((block, D), full),
                pltpu.VMEM((block, D), low),
                pltpu.VMEM((block, D), low),
                pltpu.VMEM((block, 3 * D), low),
            ],
        ),
        out_shape=[jax.ShapeDtypeStruct((rows, D), low)] * 2
        + [pltpu.VMEM(chunk_shape, dtype) for dtype in (full, low)] * FLOWS,
        compiler_params=pltpu.CompilerParams(vmem_limit_bytes=VMEM_LIMIT),
    )(me, counts, *pieces, tokens, cotangent)


def step_scale(position):
    bound_one = QKV_ROWS * LANES
    bound_two = BASE_UP * LANES
    bound_three = BASE_DOWN * LANES
    bound_four = BASE_VEC * LANES
    scale = jnp.where(
        position < bound_one,
        D ** (-0.5),
        jnp.where(
            position < bound_two,
            (D // 8) ** (-0.5),
            jnp.where(
                position < bound_three,
                D ** (-0.5),
                jnp.where(position < bound_four, FF ** (-0.5), 0.1),
            ),
        ),
    )
    decay = jnp.where(position < bound_four, 0.05, 0.0)
    return (scale, decay)


def on_device(tokens, counts, cotangent, master, first, second, rate, step):
    shard = master.shape[0]
    me = lax.axis_index(AXES)
    sizes = (lax.axis_size("wide"), lax.axis_size("narrow"))
    flows = exchange_flows(*sizes)
    rows = chunk_rows(shard)
    offset = me * shard % 1024
    own = lax.dynamic_update_slice(
        jnp.zeros((rows * LANES,), jnp.bfloat16), master.astype(jnp.bfloat16), (offset,)
    ).reshape(FLOWS, rows // FLOWS, LANES)
    pieces = gather_chunks(own, flows)
    result, grad_input, *chunks = layer(
        me.reshape(1), counts, pieces, tokens, cotangent, flows, shard
    )
    reduced = jnp.concatenate(scatter_chunks(chunks, flows), axis=0)
    reduced = lax.dynamic_slice(reduced.reshape(rows * LANES), (offset,), (shard,))
    position = me * shard + jnp.arange(shard, dtype=jnp.int32)
    first_new = 0.5 * first + 0.5 * reduced
    second_new = 0.5 * second + 0.5 * reduced * reduced
    correct = 1.0 - jnp.power(jnp.float32(0.5), step[0].astype(jnp.float32))
    scale, decay = step_scale(position)
    moved = first_new / correct / (jnp.sqrt(second_new / correct) + 1e-08)
    master_new = master - rate[0] * scale * (moved + decay * master)
    return (
        result,
        grad_input,
        master_new,
        first_new,
        second_new,
        master_new.astype(jnp.bfloat16),
    )


def solution(mesh):
    split = P(AXES)
    by_rows = P(AXES, None)
    return jax.shard_map(
        on_device,
        mesh=mesh,
        in_specs=(by_rows, split, by_rows, split, split, split, P(), P()),
        out_specs=(by_rows, by_rows, split, split, split, split),
        check_vma=False,
    )
```

```python
import functools

import jax
import jax.numpy as jnp
from jax import lax
from jax.experimental import pallas as pl
from jax.experimental.pallas import tpu as pltpu
from jax.sharding import PartitionSpec as P

D = 384
FF = 1536
HEADS = 6
HEAD_DIM = 64
PATCHES = 64
LANES = 128
PAIRS = HEADS // 2
EPS = 1e-06
AXES = ("wide", "narrow")
QKV_ROWS = 3 * D * D // LANES
OUT_ROWS = D * D // LANES
UP_ROWS = D * FF // LANES
VEC_ROWS = (6 * D + FF) // LANES
FLAT_ROWS = QKV_ROWS + OUT_ROWS + 2 * UP_ROWS + VEC_ROWS
BASE_OUT = QKV_ROWS
BASE_UP = BASE_OUT + OUT_ROWS
BASE_DOWN = BASE_UP + UP_ROWS
BASE_VEC = BASE_DOWN + UP_ROWS
VECTORS = ("gain_one", "shift_one", "bias_out", "gain_two", "shift_two", "bias_up", "bias_down")
VMEM_LIMIT = 44 * 1024 * 1024
BLOCK = 512
GROUP = 8
COLUMNS = 768
FLOWS = 2


def round_up(value, step):
    return (value + step - 1) // step * step


def dot(left, right, left_dim, right_dim):
    return lax.dot_general(
        left, right, (((left_dim,), (right_dim,)), ((), ())), preferred_element_type=jnp.float32
    )


def chunk_rows(shard):
    return round_up(shard + 1024, 16 * FLOWS * LANES) // LANES


class Flow:
    def __init__(self, rounds, devices, core):
        self.swaps = [
            [(device, device ^ pair[1 if device & core else 0]) for device in range(devices)]
            for pair in rounds
        ]
        self.core_swap = [(device, device ^ core) for device in range(devices)]
        self.core = core
        half = devices // 2
        self.across = [[0] * devices, [0] * devices]
        for side in (0, 1):
            for slot in range(half):
                for index, pair in enumerate(rounds):
                    if slot >> index & 1:
                        self.across[side][slot] ^= pair[side]
                        self.across[1 - side][half + slot] ^= pair[side]
                self.across[1 - side][half + slot] ^= core

    def owner(self, me, slot):
        side_one = (me & self.core) != 0
        return me ^ jnp.where(side_one, self.across[1][slot], self.across[0][slot])


def exchange_flows(wide, narrow):
    bits = chip_bits(wide * narrow, narrow)
    top, middle, (first, second) = bits[:1], bits[1:-2], bits[-2:]
    orders = [
        (top + [second, first] + middle, [first] + top + middle + [second]),
        (top + middle + [first, second], [second] + middle + top + [first]),
    ]
    return [Flow(list(zip(*order)), wide * narrow, narrow) for order in orders]


def chip_bits(devices, core):
    return [1 << k for k in reversed(range(devices.bit_length() - 1)) if 1 << k != core]


def after(value, other):
    if other is None:
        return value
    return lax.optimization_barrier((value, other))[0]


def gather_chunks(owns, flows):
    held = [own[None] for own in owns]
    taken = [None] * len(flows)
    turns = list(reversed(range(len(flows))))
    last = None
    for index in range(len(flows[0].swaps)):
        for turn in turns:
            if index:
                held[turn] = jnp.concatenate([after(held[turn], last), taken[turn]], axis=0)
            last = held[turn]
            taken[turn] = lax.ppermute(last, AXES, flows[turn].swaps[index])
    pieces = []
    for flow, kept, new in zip(flows, held, taken):
        pieces += [kept, new]
        pieces += [lax.ppermute(piece, AXES, flow.core_swap) for piece in (kept, new)]
    return pieces


def scatter_chunks(chunks, flows):
    parts = [
        [kept, lax.ppermute(sent, AXES, flow.core_swap)]
        for kept, sent, flow in zip(chunks[::2], chunks[1::2], flows)
    ]
    last = None
    for index in reversed(range(len(flows[0].swaps))):
        for turn, flow in enumerate(flows):
            half = parts[turn][0].shape[0] // 2
            parts[turn][0] = after(parts[turn][0], last)
            upper = sum(part[half:].astype(jnp.float32) for part in parts[turn])
            last = upper.astype(jnp.bfloat16)
            parts[turn] = [part[:half] for part in parts[turn]]
            parts[turn].append(lax.ppermute(last, AXES, flow.swaps[index]))
    return [sum(part[0].astype(jnp.float32) for part in flow) for flow in parts]


def vector_width(name):
    return FF if name == "bias_up" else D


def vector_rows():
    row = BASE_VEC
    for index, name in enumerate(VECTORS):
        for block in range(vector_width(name) // LANES):
            yield index, slice(block * LANES, (block + 1) * LANES), row
            row += 1


def matrix_blocks(matrix, base):
    height, width = matrix.shape
    blocks = width // LANES
    for block in range(blocks):
        columns = slice(block * LANES, (block + 1) * LANES)
        yield columns, pl.ds(base + block, height, stride=blocks)


def first_row(owner, shard):
    return owner * shard // 1024 * 8


def dynamic_first_row(owner, shard):
    return pl.multiple_of(lax.shift_right_logical(owner * shard, 10) * 8, 8)


def unpack(me, pieces, flows, shard, flat, w_qkv, w_out, w_up, w_down, vectors):
    rows = pieces[0].shape[1]
    devices = 4 * pieces[0].shape[0]
    sure = shard // 1024 * 8
    for owner in range(devices):
        start = first_row(owner, shard)
        flat[start : start + 8, :] = jnp.zeros((8, LANES), jnp.float32)
        flat[start + sure : start + FLOWS * rows, :] = jnp.zeros(
            (FLOWS * rows - sure, LANES), jnp.float32
        )
    for index, flow in enumerate(flows):
        low, high = index * rows, (index + 1) * rows
        cuts = sorted({low, high} | {cut for cut in (8, sure) if low < cut < high})
        for slot in range(devices):
            source = pieces[4 * index + slot * 4 // devices]
            start = dynamic_first_row(flow.owner(me, slot), shard)
            for begin, end in zip(cuts, cuts[1:]):
                piece = source[slot % source.shape[0], begin - low : end - low, :]
                piece = piece.astype(jnp.float32)
                target = (pl.ds(pl.multiple_of(start + begin, 8), end - begin), slice(None))
                if begin < 8 or begin >= sure:
                    flat[target] += piece
                else:
                    flat[target] = piece
    for matrix, base in ((w_qkv, 0), (w_out, BASE_OUT), (w_up, BASE_UP), (w_down, BASE_DOWN)):
        for columns, rows_of in matrix_blocks(matrix, base):
            matrix[:, columns] = flat[rows_of, :].astype(jnp.bfloat16)
    for index, columns, row in vector_rows():
        vectors[index : index + 1, columns] = flat[row : row + 1, :]


def pack(me, flows, shard, flat, grad_qkv, grad_out, grad_up, grad_down, vectors, outputs):
    for matrix, base in (
        (grad_qkv, 0),
        (grad_out, BASE_OUT),
        (grad_up, BASE_UP),
    ):
        for columns, rows_of in matrix_blocks(matrix, base):
            flat[rows_of, :] = matrix[:, columns]
    blocks = D // LANES
    for block in range(blocks):
        flat[pl.ds(BASE_DOWN + block, FF, stride=blocks), :] = grad_down[
            block * LANES : (block + 1) * LANES, :
        ].T
    for index, columns, row in vector_rows():
        flat[row : row + 1, :] = vectors[index : index + 1, columns]
    flat[FLAT_ROWS:, :] = jnp.zeros((flat.shape[0] - FLAT_ROWS, LANES), jnp.float32)
    for index, flow in enumerate(flows):
        kept, sent = outputs[2 * index : 2 * index + 2]
        half, rows, _ = kept.shape
        for slot in range(half):
            start = dynamic_first_row(flow.owner(me, slot), shard) + index * rows
            kept[slot] = flat[pl.ds(pl.multiple_of(start, 8), rows), :]
            start = dynamic_first_row(flow.owner(me, half + slot), shard) + index * rows
            sent[slot] = flat[pl.ds(pl.multiple_of(start, 8), rows), :].astype(jnp.bfloat16)


def vector(vectors, name):
    index = VECTORS.index(name)
    return vectors[index : index + 1, : vector_width(name)]


def normalize(values):
    center = values - jnp.mean(values, axis=-1, keepdims=True)
    spread = jnp.mean(center * center, axis=-1, keepdims=True)
    scale = lax.rsqrt(spread + EPS)
    return center * scale, scale


def norm_back(grad, gain, hat, scale):
    inner = grad * gain
    mean_inner = jnp.mean(inner, axis=-1, keepdims=True)
    mean_cross = jnp.mean(inner * hat, axis=-1, keepdims=True)
    return scale * (inner - mean_inner - hat * mean_cross)


def first_halves():
    return lax.broadcasted_iota(jnp.int32, (PATCHES, LANES), 1) < HEAD_DIM


def block_diagonal(values, first_half):
    zero = jnp.zeros_like(values)
    return jnp.concatenate(
        [jnp.where(first_half, values, zero), jnp.where(first_half, zero, values)], axis=0
    )


def own_halves(values, first_half):
    return jnp.where(first_half, values[:PATCHES], values[PATCHES:])


def head_chains(samples):
    for sample in range(0, samples, GROUP):
        yield [
            (slice(each * PATCHES, (each + 1) * PATCHES), pair * LANES, each)
            for each in range(sample, min(sample + GROUP, samples))
            for pair in range(PAIRS)
        ]


def attention(count, packed, chance, mixed):
    first_half = first_halves()
    slots = lax.broadcasted_iota(jnp.int32, (PATCHES, LANES), 0)
    for chains in head_chains(packed.shape[0] // PATCHES):
        scores = [
            dot(
                packed[rows, D + at : D + at + LANES],
                block_diagonal(packed[rows, at : at + LANES], first_half),
                1,
                1,
            )
            for rows, at, _ in chains
        ]
        scores = [
            jnp.where(slots < count(each), score * HEAD_DIM**-0.5, -1e30)
            for score, (_, _, each) in zip(scores, chains)
        ]
        exponents = [jnp.exp(score - jnp.max(score, axis=0, keepdims=True)) for score in scores]
        attends = [
            exponent * (1.0 / jnp.sum(exponent, axis=0, keepdims=True)) for exponent in exponents
        ]
        for attend, (rows, at, _) in zip(attends, chains):
            chance[rows, at : at + LANES] = attend
        mixes = [
            dot(attend.astype(jnp.bfloat16), packed[rows, 2 * D + at : 2 * D + at + LANES], 0, 0)
            for attend, (rows, at, _) in zip(attends, chains)
        ]
        for mix, (rows, at, _) in zip(mixes, chains):
            mixed[rows, at : at + LANES] = own_halves(mix, first_half).astype(jnp.bfloat16)


def attention_back(packed, chance, grad_mixed, grad_packed):
    first_half = first_halves()
    factor = HEAD_DIM**-0.5
    for chains in head_chains(packed.shape[0] // PATCHES):
        sides = [
            block_diagonal(grad_mixed[rows, at : at + LANES], first_half) for rows, at, _ in chains
        ]
        grad_attends = [
            dot(packed[rows, 2 * D + at : 2 * D + at + LANES], side, 1, 1)
            for side, (rows, at, _) in zip(sides, chains)
        ]
        attends = [chance[rows, at : at + LANES] for rows, at, _ in chains]
        grad_values = [
            dot(attend.astype(jnp.bfloat16), side, 1, 0) for attend, side in zip(attends, sides)
        ]
        for grad, (rows, at, _) in zip(grad_values, chains):
            grad_packed[rows, 2 * D + at : 2 * D + at + LANES] = grad.astype(jnp.bfloat16)
        inners = [
            jnp.sum(attend * grad, axis=0, keepdims=True)
            for attend, grad in zip(attends, grad_attends)
        ]
        grad_scores = [
            (attend * (grad - inner)).astype(jnp.bfloat16)
            for attend, grad, inner in zip(attends, grad_attends, inners)
        ]
        grad_keys = [
            dot(grad, block_diagonal(packed[rows, at : at + LANES], first_half), 1, 0) * factor
            for grad, (rows, at, _) in zip(grad_scores, chains)
        ]
        for grad, (rows, at, _) in zip(grad_keys, chains):
            grad_packed[rows, D + at : D + at + LANES] = grad.astype(jnp.bfloat16)
        grad_queries = [
            dot(grad, packed[rows, D + at : D + at + LANES], 0, 0)
            for grad, (rows, at, _) in zip(grad_scores, chains)
        ]
        for grad, (rows, at, _) in zip(grad_queries, chains):
            grad_packed[rows, at : at + LANES] = (own_halves(grad, first_half) * factor).astype(
                jnp.bfloat16
            )


def layer_kernel(flows, shard, *refs):
    me, counts = refs[:2]
    pieces = refs[2 : 2 + 4 * FLOWS]
    tokens, cotangent, result, grad_input = refs[2 + 4 * FLOWS : 6 + 4 * FLOWS]
    outputs = refs[6 + 4 * FLOWS : 6 + 6 * FLOWS]
    (
        flat,
        w_qkv,
        w_out,
        w_up,
        w_down,
        vectors,
        acc_qkv,
        acc_out,
        acc_up,
        acc_down,
        acc_vectors,
        packed,
        chance,
        mixed,
        grad_mixed,
        grad_packed,
    ) = refs[6 + 6 * FLOWS :]
    step = pl.program_id(0)
    samples = tokens.shape[0] // PATCHES

    @pl.when(step == 0)
    def _():
        unpack(me[0], pieces, flows, shard, flat, w_qkv, w_out, w_up, w_down, vectors)
        for ref in (acc_qkv, acc_out, acc_up, acc_down, acc_vectors):
            ref[...] = jnp.zeros_like(ref)

    def count(sample):
        return counts[step * samples + sample]

    def add_vector(name, values, at=0):
        index = VECTORS.index(name)
        acc_vectors[index : index + 1, at : at + values.shape[1]] += jnp.sum(
            values, axis=0, keepdims=True
        )

    inputs = tokens[...].astype(jnp.float32)
    hat_one, scale_one = normalize(inputs)
    gain_one = vector(vectors, "gain_one")
    normed_one = (hat_one * gain_one + vector(vectors, "shift_one")).astype(jnp.bfloat16)
    packed[...] = dot(normed_one, w_qkv[...], 1, 0).astype(jnp.bfloat16)
    attention(count, packed, chance, mixed)
    hidden = inputs + dot(mixed[...], w_out[...], 1, 0) + vector(vectors, "bias_out")

    hat_two, scale_two = normalize(hidden)
    gain_two = vector(vectors, "gain_two")
    normed_two = (hat_two * gain_two + vector(vectors, "shift_two")).astype(jnp.bfloat16)
    slots = lax.broadcasted_iota(jnp.int32, (PATCHES, 1), 0)
    visible = jnp.concatenate(
        [jnp.where(slots < count(sample), 1.0, 0.0) for sample in range(samples)], axis=0
    )
    grad_out = cotangent[...].astype(jnp.float32) * visible
    grad_out_low = grad_out.astype(jnp.bfloat16)
    add_vector("bias_down", grad_out)
    total = hidden + vector(vectors, "bias_down")
    grad_normed_two = jnp.zeros_like(hidden)
    bias_up = vector(vectors, "bias_up")
    for at in range(0, FF, COLUMNS):
        columns = slice(at, at + COLUMNS)
        upward = dot(normed_two, w_up[:, columns], 1, 0) + bias_up[:, columns]
        below = 0.5 * (1.0 + lax.erf(upward * 0.5**0.5))
        active = (upward * below).astype(jnp.bfloat16)
        slope = below + upward * (jnp.exp(-0.5 * upward * upward) * (0.5 / jnp.pi) ** 0.5)
        total = total + dot(active, w_down[columns, :], 1, 0)
        grad_upward = dot(grad_out_low, w_down[columns, :], 1, 1) * slope
        grad_upward = grad_upward.astype(jnp.bfloat16)
        add_vector("bias_up", grad_upward.astype(jnp.float32), at)
        acc_down[:, columns] += dot(grad_out_low, active, 0, 0)
        acc_up[:, columns] += dot(normed_two, grad_upward, 0, 0)
        grad_normed_two = grad_normed_two + dot(grad_upward, w_up[:, columns], 1, 1)
    result[...] = total.astype(jnp.bfloat16)
    add_vector("gain_two", grad_normed_two * hat_two)
    add_vector("shift_two", grad_normed_two)
    grad_hidden = grad_out + norm_back(grad_normed_two, gain_two, hat_two, scale_two)

    grad_hidden_low = grad_hidden.astype(jnp.bfloat16)
    add_vector("bias_out", grad_hidden_low.astype(jnp.float32))
    acc_out[...] += dot(mixed[...], grad_hidden_low, 0, 0)
    grad_mixed[...] = dot(grad_hidden_low, w_out[...], 1, 1).astype(jnp.bfloat16)
    attention_back(packed, chance, grad_mixed, grad_packed)
    acc_qkv[...] += dot(normed_one, grad_packed[...], 0, 0)
    grad_normed_one = dot(grad_packed[...], w_qkv[...], 1, 1)
    add_vector("gain_one", grad_normed_one * hat_one)
    add_vector("shift_one", grad_normed_one)
    grad_input[...] = (
        grad_hidden + norm_back(grad_normed_one, gain_one, hat_one, scale_one)
    ).astype(jnp.bfloat16)

    @pl.when(step == pl.num_programs(0) - 1)
    def _():
        pack(
            me[0], flows, shard, flat, acc_qkv, acc_out, acc_up, acc_down, acc_vectors, outputs
        )


def layer(me, counts, pieces, tokens, cotangent, flows, shard):
    rows = tokens.shape[0]
    block = min(BLOCK, rows)
    quarter, piece_rows, _ = pieces[0].shape
    devices = 4 * quarter
    flat_rows = first_row(devices - 1, shard) + FLOWS * piece_rows
    low = jnp.bfloat16
    full = jnp.float32

    def by_rows():
        return pl.BlockSpec((block, D), lambda i, me, counts: (i, 0))

    chunk_shape = (devices // 2, piece_rows, LANES)
    return pl.pallas_call(
        functools.partial(layer_kernel, flows, shard),
        name="layer",
        grid_spec=pltpu.PrefetchScalarGridSpec(
            num_scalar_prefetch=2,
            grid=(rows // block,),
            in_specs=[pl.BlockSpec(memory_space=pltpu.VMEM)] * len(pieces)
            + [by_rows(), by_rows()],
            out_specs=[by_rows(), by_rows()]
            + [pl.BlockSpec(memory_space=pltpu.VMEM)] * (2 * FLOWS),
            scratch_shapes=[
                pltpu.VMEM((flat_rows, LANES), full),
                pltpu.VMEM((D, 3 * D), low),
                pltpu.VMEM((D, D), low),
                pltpu.VMEM((D, FF), low),
                pltpu.VMEM((FF, D), low),
                pltpu.VMEM((8, FF), full),
                pltpu.VMEM((D, 3 * D), full),
                pltpu.VMEM((D, D), full),
                pltpu.VMEM((D, FF), full),
                pltpu.VMEM((D, FF), full),
                pltpu.VMEM((8, FF), full),
                pltpu.VMEM((block, 3 * D), low),
                pltpu.VMEM((block, D), full),
                pltpu.VMEM((block, D), low),
                pltpu.VMEM((block, D), low),
                pltpu.VMEM((block, 3 * D), low),
            ],
        ),
        out_shape=[jax.ShapeDtypeStruct((rows, D), low)] * 2
        + [pltpu.VMEM(chunk_shape, dtype) for dtype in (full, low)] * FLOWS,
        compiler_params=pltpu.CompilerParams(vmem_limit_bytes=VMEM_LIMIT),
    )(me, counts, *pieces, tokens, cotangent)


def step_scale(position):
    bound_one = QKV_ROWS * LANES
    bound_two = BASE_UP * LANES
    bound_three = BASE_DOWN * LANES
    bound_four = BASE_VEC * LANES
    scale = jnp.where(
        position < bound_one,
        D ** (-0.5),
        jnp.where(
            position < bound_two,
            (D // 8) ** (-0.5),
            jnp.where(
                position < bound_three,
                D ** (-0.5),
                jnp.where(position < bound_four, FF ** (-0.5), 0.1),
            ),
        ),
    )
    decay = jnp.where(position < bound_four, 0.05, 0.0)
    return (scale, decay)


def on_device(tokens, counts, cotangent, master, first, second, rate, step):
    shard = master.shape[0]
    me = lax.axis_index(AXES)
    sizes = (lax.axis_size("wide"), lax.axis_size("narrow"))
    flows = exchange_flows(*sizes)
    rows = chunk_rows(shard)
    offset = me * shard % 1024
    own = lax.dynamic_update_slice(
        jnp.zeros((rows * LANES,), jnp.bfloat16), master.astype(jnp.bfloat16), (offset,)
    ).reshape(FLOWS, rows // FLOWS, LANES)
    pieces = gather_chunks(own, flows)
    result, grad_input, *chunks = layer(
        me.reshape(1), counts, pieces, tokens, cotangent, flows, shard
    )
    reduced = jnp.concatenate(scatter_chunks(chunks, flows), axis=0)
    reduced = lax.dynamic_slice(reduced.reshape(rows * LANES), (offset,), (shard,))
    position = me * shard + jnp.arange(shard, dtype=jnp.int32)
    first_new = 0.5 * first + 0.5 * reduced
    second_new = 0.5 * second + 0.5 * reduced * reduced
    correct = 1.0 - jnp.power(jnp.float32(0.5), step[0].astype(jnp.float32))
    scale, decay = step_scale(position)
    moved = first_new / correct / (jnp.sqrt(second_new / correct) + 1e-08)
    master_new = master - rate[0] * scale * (moved + decay * master)
    return (
        result,
        grad_input,
        master_new,
        first_new,
        second_new,
        master_new.astype(jnp.bfloat16),
    )


def solution(mesh):
    split = P(AXES)
    by_rows = P(AXES, None)
    return jax.shard_map(
        on_device,
        mesh=mesh,
        in_specs=(by_rows, split, by_rows, split, split, split, P(), P()),
        out_specs=(by_rows, by_rows, split, split, split, split),
        check_vma=False,
    )
```
